32 devices in a mesh: grp: 4 (over z), dev: 8 (over y, x, core).
Axes of the slice: x: 2, y: 2, z: 4, core: 2. Of those that a mesh axis runs over, the one named last changes fastest.
Arguments:
- stamps: int32 [65536], P(('grp', 'dev')), may hold values from 0 to 14399, as said below
- account: int32 [65536], P(('grp', 'dev')), may hold values from 0 to 15, as said below
- kind: int32 [65536], P(('grp', 'dev')), may hold values from 0 to 5
- weight: bfloat16 [65536], P(('grp', 'dev')), may hold values from -3 to 3
- used: int32 [32, 64], P(('grp', 'dev')), may hold values from 1 to 32, as said below
Outputs:
- pair_profile: float32 [36, 1024], P(None, 'dev')
- triple_profile: float32 [8, 1024], P(None, 'dev')
The draws below stay inside these ranges and needn't reach their ends.
Inputs may be any that keep to these rules, and one draw needn't show every extreme that they name: `account`: small values are more common. `stamps`: an event of sender r lies in time range r // 8: its stamp is at least (r // 8) * 3600 and below that plus 3600. `used`: column 0 of every row equals 32.
All inputs are finite; a program needn't handle non-finite values.
Results may differ from the reference program's by a relative error of at most 0.0003.
Values sent between devices are 32-bit elements; how exact they have to be, the bound alone decides.
A program may use at most 64 MiB of HBM per device.

```python
import jax
import jax.numpy as jnp
from jax import lax

DELTA = 3600
BLK = 256
ACC_BLK = 16
NB = 8
CAP = 32
ACCOUNTS = 1024
EVENTS = 65536
N_GRP = 4
N_DEV = 8


def draw_stamps(key, part):
    index = jnp.arange(EVENTS, dtype=jnp.int32)
    group = index // (N_DEV * NB * BLK)
    offset = jax.random.randint(key, (EVENTS,), 0, DELTA, dtype=jnp.int32)
    return offset + group * DELTA


def draw_account(key, part):
    first = jax.random.randint(jax.random.fold_in(key, 1), (EVENTS,), 0, ACC_BLK, dtype=jnp.int32)
    second = jax.random.randint(jax.random.fold_in(key, 2), (EVENTS,), 0, ACC_BLK, dtype=jnp.int32)
    return jnp.minimum(first, second)


def draw_used(key, part):
    counts = jax.random.randint(key, (N_GRP * N_DEV, N_DEV * NB), 1, CAP + 1, dtype=jnp.int32)
    return counts.at[:, 0].set(CAP)


def with_ends(drawn, stream_key, smallest, top_value):
    longest = drawn.shape.index(max(drawn.shape))
    spots = []
    for shift in (0, 1):
        where = [jax.random.randint(jax.random.fold_in(stream_key, axis), (), 0, length) for axis, length in enumerate(drawn.shape)]
        where[longest] = (where[longest] + shift) % drawn.shape[longest]
        spots.append(tuple(where))
    return drawn.at[spots[0]].set(smallest).at[spots[1]].set(top_value)


def level_of(rng, extent, cuts, smallest, largest):
    def one(position, shards_of):
        steps = jax.random.uniform(jax.random.fold_in(jax.random.fold_in(rng, 6), position), (shards_of,), jnp.float32, smallest / len(cuts), largest / len(cuts))
        return jnp.repeat(jnp.exp(steps), extent[position] // shards_of).reshape((-1,) + (1,) * (len(extent) - position - 1))

    loudness = one(*cuts[0])
    for cut in cuts[1:]:
        loudness = loudness * one(*cut)
    return loudness


def bell_draw(key, extent, scale, most, split=(), held_as=jnp.bfloat16):
    gain = level_of(key, extent, split, -0.22, 0.18) if split else 1.0
    values = jax.random.normal(key, extent, jnp.float32) * scale * gain
    return jnp.minimum(jnp.maximum(values, -most), most).astype(held_as)


def setup_inputs(seed: int = 0) -> dict:
    keys = jax.random.split(jax.random.key(seed), 6)
    return {
        "stamps": draw_stamps(jax.random.fold_in(keys[5], 71), 0),
        "account": draw_account(jax.random.fold_in(keys[5], 71), 0),
        "kind": with_ends(jax.random.randint(keys[2], (EVENTS,), 0, 6), jax.random.fold_in(keys[2], 1), 0, 5).astype(jnp.int32),
        "weight": bell_draw(keys[3], (EVENTS,), 0.5, 3.0, ((0, 32),)),
        "used": draw_used(jax.random.fold_in(keys[5], 71), 0),
    }


def count_block(own_rows, prior_rows):
    fields = jnp.concatenate([prior_rows, own_rows], axis=1)
    stamp, local, kinds, wt = fields[0], fields[1], fields[2], fields[3]
    blk = own_rows.shape[1]
    gap = stamp[None, :] - stamp[:, None]
    linked = (local[:, None] == local[None, :]) & (gap > 0.0) & (gap <= DELTA)
    link_all = linked.astype(jnp.float32)
    link_own = link_all[:, blk:]
    classes = (kinds[:, None] == jnp.arange(6).astype(jnp.float32)[None, :]).astype(jnp.float32) * wt[:, None]
    earlier = jnp.dot(link_own.T, classes, precision=lax.Precision.HIGHEST)
    later = classes[blk:]
    pair_terms = (earlier[:, :, None] * later[:, None, :]).reshape(blk, 36)
    owners_hot = (local[blk:, None] == jnp.arange(ACC_BLK).astype(jnp.float32)[None, :]).astype(jnp.float32)
    pairs = jnp.dot(pair_terms.T, owners_hot, precision=lax.Precision.HIGHEST)
    dirs = jnp.stack([wt * (kinds < 2.5), wt * (kinds > 2.5)], axis=0)
    weighted = (link_all[None, :, :] * dirs[:, None, :]).reshape(2 * 2 * blk, 2 * blk)
    middle = jnp.dot(weighted, link_own, precision=lax.Precision.HIGHEST).reshape(2, 2 * blk, blk)
    closed = middle * link_own[None]
    ends = jnp.einsum('ai,bik->abk', dirs, closed, precision=lax.Precision.HIGHEST)
    last = dirs[:, blk:]
    triple_terms = (ends[:, :, None, :] * last[None, None, :, :]).reshape(8, blk)
    triples = jnp.dot(triple_terms, owners_hot, precision=lax.Precision.HIGHEST)
    return pairs, triples


def reference(stamps, account, kind, weight, used):
    shape5 = (N_GRP, N_DEV, N_DEV, NB, CAP)
    live = used.reshape(N_GRP, N_DEV, N_DEV, NB)[..., None] > jnp.arange(CAP).astype(jnp.int32)
    wt = jnp.where(live, weight.reshape(shape5).astype(jnp.float32), jnp.float32(0.0))
    fields = [stamps.reshape(shape5).astype(jnp.float32),
              account.reshape(shape5).astype(jnp.float32),
              kind.reshape(shape5).astype(jnp.float32), wt]
    arranged = [f.transpose(0, 2, 3, 1, 4).reshape(N_GRP, N_DEV, NB, BLK) for f in fields]
    stacked = jnp.stack(arranged, axis=3)
    prior = jnp.concatenate([jnp.zeros_like(stacked[:1]), stacked[:-1]], axis=0)
    total = N_GRP * N_DEV * NB
    batch = 1
    for cand in (16, 8, 4, 2):
        if total % cand == 0:
            batch = cand
            break
    own_b = stacked.reshape(total // batch, batch, 4, BLK)
    prior_b = prior.reshape(total // batch, batch, 4, BLK)
    pairs, triples = lax.map(lambda xs: jax.vmap(count_block)(xs[0], xs[1]), (own_b, prior_b))
    pairs = pairs.reshape(N_GRP, N_DEV, NB, 36, ACC_BLK).sum(axis=0)
    triples = triples.reshape(N_GRP, N_DEV, NB, 8, ACC_BLK).sum(axis=0)
    pair_profile = pairs.transpose(2, 0, 1, 3).reshape(36, ACCOUNTS)
    triple_profile = triples.transpose(2, 0, 1, 3).reshape(8, ACCOUNTS)
    return (pair_profile, triple_profile)
```

```python
import functools

import jax
import jax.numpy as jnp
from jax import lax
from jax.experimental import pallas as pl
from jax.experimental.pallas import tpu as pltpu
from jax.sharding import PartitionSpec as P

DELTA = 3600
ACC_BLK = 16
LANES = 128
ACC_STEP = 8192.0
HALF_SPAN = 2048.0
FIELDS = 4
ROWS = 48
MESH = pl.DeviceIdType.MESH


def iota(shape, dim):
    return lax.broadcasted_iota(jnp.int32, shape, dim)


def split(x):
    high = x.astype(jnp.bfloat16)
    return high, (x - high.astype(jnp.float32)).astype(jnp.bfloat16)


def matmul(a, b):
    return jnp.dot(a, b, preferred_element_type=jnp.float32)


def matmul_t(a, b):
    return lax.dot_general(a, b, (((1,), (1,)), ((), ())), preferred_element_type=jnp.float32)


def by_block(x, slots):
    senders = x.shape[0]
    per_row = LANES // slots
    row, place = iota(x.shape, 0), iota(x.shape, 1) // slots
    out = x
    for r in range(1, per_row):
        moved = pltpu.roll(pltpu.roll(x, r * slots, 1), (senders - r) % senders, 0)
        out = jnp.where((row + r - place) % per_row == 0, moved, out)
    return out


class Events:
    def __init__(self, ref, slots, rows_per_field):
        self.keys, self.kinds, self.weights, self.columns = [], [], [], []
        self.per_row = LANES // slots
        self.rows = ref.shape[0] // self.per_row
        for h in range(rows_per_field):
            stamp, account, kind, weight = (ref[:, f * rows_per_field + h, :] for f in range(FIELDS))
            key = by_block(account * ACC_STEP + stamp, slots)
            self.keys.append(key)
            self.kinds.append(by_block(kind, slots))
            self.weights.append(by_block(weight, slots))
            self.columns.append(jnp.transpose(key))

    def at(self, b):
        h, q = divmod(b, self.per_row)
        places = [q + self.per_row * t for t in range(self.rows)]

        def row(field):
            return jnp.concatenate([field[h][p : p + 1, :] for p in places], axis=1)

        column = jnp.concatenate([self.columns[h][:, p : p + 1] for p in places], axis=0)
        return row(self.keys), column, row(self.kinds), row(self.weights)


def within(row, column):
    return jnp.where(jnp.abs(row - column) < HALF_SPAN, 1.0, 0.0).astype(jnp.bfloat16)


def pick(code, wanted, weight):
    return jnp.where(code == wanted.astype(jnp.float32), weight, 0.0)


def kernel(
    n_grp, n_dev, blocks, slots,
    stamp_ref, account_ref, kind_ref, weight_ref, used_ref, out_ref,
    stamp_in, account_in, kind_in, weight_in, used_in, send, own, prior, early, part,
    in_sem, send_sem, prior_send_sem, own_sem, prior_sem, part_send_sem, part_sem,
):
    g, d = lax.axis_index("grp"), lax.axis_index("dev")
    width = slots * blocks
    rows_per_field = max(1, width // LANES)
    per_row = LANES // slots

    loads = [
        pltpu.make_async_copy(src, dst, in_sem.at[i])
        for i, (src, dst) in enumerate(
            [(stamp_ref, stamp_in), (account_ref, account_in), (kind_ref, kind_in), (weight_ref, weight_in), (used_ref, used_in)]
        )
    ]
    for load in loads:
        load.start()

    barrier = pltpu.get_barrier_semaphore()

    def greet(grp, dev):
        pl.semaphore_signal(barrier, inc=1, device_id={"grp": grp, "dev": dev}, device_id_type=MESH)

    for k in range(1, n_dev):
        greet(g, lax.rem(d + k, n_dev))

    @pl.when(g > 0)
    def _():
        for k in range(1, n_dev):
            greet(g - 1, lax.rem(d + k, n_dev))

    for k in range(1, n_grp):
        greet(lax.rem(g + k, n_grp), d)

    for load in loads:
        load.wait()

    n_used = used_in.shape[1]
    shape = stamp_in.shape
    counts = jnp.broadcast_to(used_in[...].astype(jnp.float32), (shape[0], n_used))
    counts = jnp.where(iota(counts.shape, 1) // per_row == iota(counts.shape, 0), counts, 0.0)
    spread = jnp.where(iota((n_used, LANES), 0) % per_row == iota((n_used, LANES), 1) // slots, 1.0, 0.0)
    live_slots = matmul(counts.astype(jnp.bfloat16), spread.astype(jnp.bfloat16))
    live = (iota(shape, 1) % slots).astype(jnp.float32) < live_slots
    fields = [
        (stamp_in[...] - g * DELTA).astype(jnp.float32),
        account_in[...].astype(jnp.float32),
        kind_in[...].astype(jnp.float32),
        jnp.where(live, weight_in[...].astype(jnp.float32), 0.0),
    ]
    for f, field in enumerate(fields):
        for shift in range(max(1, LANES // width)):
            moved = pltpu.roll(field, LANES - shift * width, 1) if shift else field
            for o in range(shift, n_dev, max(1, LANES // width)):
                at = o * width // LANES
                send[o, f * rows_per_field : (f + 1) * rows_per_field, :] = moved[at : at + rows_per_field, :]
    own[d] = send[d]

    @pl.when(g < n_grp - 1)
    def _():
        pl.semaphore_wait(barrier, 2 * (n_dev - 1) + n_grp - 1)

    @pl.when(g == n_grp - 1)
    def _():
        pl.semaphore_wait(barrier, n_dev - 1 + n_grp - 1)

    for k in range(1, n_dev):
        to = lax.rem(d + k, n_dev)
        pltpu.make_async_remote_copy(
            send.at[to], own.at[d], send_sem, own_sem, device_id={"grp": g, "dev": to}, device_id_type=MESH
        ).start()

    @pl.when(g < n_grp - 1)
    def _():
        for k in range(n_dev):
            to = lax.rem(d + k, n_dev)
            pltpu.make_async_remote_copy(
                send.at[to], prior.at[d], prior_send_sem, prior_sem, device_id={"grp": g + 1, "dev": to}, device_id_type=MESH
            ).start()

    def done(ref, count, sem):
        some = ref.at[pl.ds(0, count)]
        pltpu.make_async_copy(some, some, sem).wait()

    size = slots * n_dev
    row40, row8 = iota((40, size), 0), iota((8, size), 0)

    done(own, n_dev - 1, own_sem)
    mine = Events(own, slots, rows_per_field)
    for b in range(blocks):
        key, column, kind, weight = mine.at(b)
        turn = jnp.where(kind > 2.5, 1.0, 0.0)
        link = within(key - HALF_SPAN, column)
        second = pick(turn, row8 // 2 % 2, weight)
        left = jnp.concatenate([pick(kind, row40 // 6, weight), second, pick(turn, row8 // 4, weight)], axis=0)
        sums = matmul(left.astype(jnp.bfloat16), link)
        high, low = split(second * sums[48:56])
        inner = matmul(jnp.concatenate([high, low], axis=0), link)
        early[b, 0:48, :] = sums[0:48]
        early[b, 48:56, :] = inner[0:8] + inner[8:16]

    @pl.when(g > 0)
    def _():
        done(prior, n_dev, prior_sem)

    @pl.when(g == 0)
    def _():
        prior[...] = jnp.zeros_like(prior)

    before = Events(prior, slots, rows_per_field)
    total = jnp.zeros((ROWS, LANES), jnp.float32)
    for b in range(blocks):
        key, _, kind, weight = mine.at(b)
        turn = jnp.where(kind > 2.5, 1.0, 0.0)
        p_key, p_column, p_kind, p_weight = before.at(b)
        p_turn = jnp.where(p_kind > 2.5, 1.0, 0.0)
        later = matmul(pick(p_turn, row8 // 2 % 2, p_weight).astype(jnp.bfloat16), within(p_key + HALF_SPAN, p_column))
        first = pick(p_turn, row8 // 4, p_weight)
        high, low = split(first * later)
        left = jnp.concatenate([pick(p_kind, row40 // 6, p_weight), first], axis=0).astype(jnp.bfloat16)
        sums = matmul(jnp.concatenate([left, high, low], axis=0), within(key + (HALF_SPAN - 0.5), p_column))
        pairs = (early[b, 0:40, :] + sums[0:40]) * pick(kind, row40 % 6, jnp.where(row40 < 36, weight, 0.0))
        inner = early[b, 48:56, :] + (sums[48:56] + sums[56:64]) + sums[40:48] * early[b, 40:48, :]
        triples = inner * pick(turn, row8 % 2, weight)
        high, low = split(jnp.concatenate([pairs, triples], axis=0))
        account = jnp.floor(key * (1.0 / ACC_STEP)) + float(b * ACC_BLK)
        mark = jnp.where(account == iota((LANES, size), 0).astype(jnp.float32), 1.0, 0.0).astype(jnp.bfloat16)
        profile = matmul_t(jnp.concatenate([high, low], axis=0), mark)
        total = total + (profile[0:ROWS] + profile[ROWS:])

    part[g] = total
    for k in range(1, n_grp):
        pltpu.make_async_remote_copy(
            part.at[g], part.at[g], part_send_sem, part_sem,
            device_id={"grp": lax.rem(g + k, n_grp), "dev": d}, device_id_type=MESH,
        ).start()
    done(part, n_grp - 1, part_sem)
    result = part[0]
    for k in range(1, n_grp):
        result = result + part[k]
    out_ref[...] = result
    done(send, n_dev - 1, send_sem)
    done(part, n_grp - 1, part_send_sem)

    @pl.when(g < n_grp - 1)
    def _():
        done(send, n_dev, prior_send_sem)


def write_out(profile_ref, pair_ref, triple_ref, sems):
    pairs = pltpu.make_async_copy(profile_ref.at[pl.ds(0, 36)], pair_ref, sems.at[0])
    triples = pltpu.make_async_copy(profile_ref.at[pl.ds(40, 8)], triple_ref, sems.at[1])
    pairs.start()
    triples.start()
    pairs.wait()
    triples.wait()


def per_device(stamps, account, kind, weight, used):
    n_grp, n_dev = lax.axis_size("grp"), lax.axis_size("dev")
    blocks = used.shape[1] // n_dev
    slots = stamps.shape[0] // (n_dev * blocks)
    rows = stamps.shape[0] // LANES
    chunk = FIELDS * max(1, slots * blocks // LANES)
    anywhere = pl.BlockSpec(memory_space=pl.ANY)
    vmem = pl.BlockSpec(memory_space=pltpu.VMEM)
    f32 = jnp.float32
    profile = pl.pallas_call(
        functools.partial(kernel, n_grp, n_dev, blocks, slots),
        out_shape=pltpu.VMEM((ROWS, LANES), f32),
        in_specs=[anywhere] * 5,
        out_specs=vmem,
        scratch_shapes=[
            pltpu.VMEM((rows, LANES), jnp.int32),
            pltpu.VMEM((rows, LANES), jnp.int32),
            pltpu.VMEM((rows, LANES), jnp.int32),
            pltpu.VMEM((rows, LANES), jnp.bfloat16),
            pltpu.VMEM(used.shape, jnp.int32),
            pltpu.VMEM((n_dev, chunk, LANES), f32),
            pltpu.VMEM((n_dev, chunk, LANES), f32),
            pltpu.VMEM((n_dev, chunk, LANES), f32),
            pltpu.VMEM((blocks, 56, slots * n_dev), f32),
            pltpu.VMEM((n_grp, ROWS, LANES), f32),
            pltpu.SemaphoreType.DMA((5,)),
        ]
        + [pltpu.SemaphoreType.DMA] * 6,
        compiler_params=pltpu.CompilerParams(collective_id=0, has_side_effects=True),
    )(*(x.reshape(rows, LANES) for x in (stamps, account, kind, weight)), used)
    return tuple(
        pl.pallas_call(
            write_out,
            out_shape=[jax.ShapeDtypeStruct((36, LANES), f32), jax.ShapeDtypeStruct((8, LANES), f32)],
            in_specs=[vmem],
            out_specs=[anywhere] * 2,
            scratch_shapes=[pltpu.SemaphoreType.DMA((2,))],
        )(pltpu.with_memory_space_constraint(profile, pltpu.VMEM))
    )


def solution(mesh):
    return jax.shard_map(
        per_device,
        mesh=mesh,
        in_specs=(
            P(("grp", "dev")),
            P(("grp", "dev")),
            P(("grp", "dev")),
            P(("grp", "dev")),
            P(("grp", "dev"), None),
        ),
        out_specs=(P(None, "dev"), P(None, "dev")),
        check_vma=False,
    )
```

```python
import functools

import jax
import jax.numpy as jnp
from jax import lax
from jax.experimental import pallas as pl
from jax.experimental.pallas import tpu as pltpu
from jax.sharding import PartitionSpec as P

DELTA = 3600
ACC_BLK = 16
LANES = 128
STEP = 4096
FIELDS = 4
ROWS = 48
MESH = pl.DeviceIdType.MESH
BF16, F32, I16 = jnp.bfloat16, jnp.float32, jnp.int16


def iota(shape, dim):
    return lax.broadcasted_iota(jnp.int32, shape, dim)


def matmul(a, b):
    return jnp.dot(a, b, preferred_element_type=F32)


def matmul_t(a, b):
    return lax.dot_general(a, b, (((1,), (1,)), ((), ())), preferred_element_type=F32)


def split(x):
    high = x.astype(BF16)
    return jnp.concatenate([high, (x - high.astype(F32)).astype(BF16)], axis=0)


def by_block(x, slots):
    senders = x.shape[0]
    per_row = LANES // slots
    row, place = iota(x.shape, 0), iota(x.shape, 1) // slots
    out = x
    for r in range(1, per_row):
        moved = pltpu.roll(pltpu.roll(x, r * slots, 1), (senders - r) % senders, 0)
        out = jnp.where((row + r - place) % per_row == 0, moved, out)
    return out


def peers(count, body):
    if count <= 64:
        for k in range(1, count):
            body(k)
    else:
        lax.fori_loop(1, count, lambda k, _: body(k), None)


def kernel(
    n_grp, n_dev, blocks, slots,
    stamp_ref, account_ref, kind_ref, weight_ref, used_ref, out_ref,
    stamp_in, account_in, kind_in, weight_in, used_in, send, events, columns, lefts, sums_in, sums_out, marks, profile,
    in_sem, send_sem, event_sem,
):
    g, d = lax.axis_index("grp"), lax.axis_index("dev")
    me = g * n_dev + d
    width = slots * blocks
    rows_per_field = max(1, width // LANES)
    per_row = LANES // slots
    size = slots * n_dev
    devices = n_grp * n_dev

    loads = [
        pltpu.make_async_copy(src, dst, in_sem.at[i])
        for i, (src, dst) in enumerate(
            [(stamp_ref, stamp_in), (account_ref, account_in), (kind_ref, kind_in), (weight_ref, weight_in), (used_ref, used_in)]
        )
    ]
    for load in loads:
        load.start()

    def place(k):
        to = lax.rem(me + k, devices)
        return to // n_dev, lax.rem(to, n_dev)

    barrier = pltpu.get_barrier_semaphore()

    def greet(k):
        grp, dev = place(k)
        pl.semaphore_signal(barrier, inc=1, device_id={"grp": grp, "dev": dev}, device_id_type=MESH)

    peers(devices, greet)
    for load in loads:
        load.wait()

    n_used = used_in.shape[1]
    shape = stamp_in.shape
    counts = jnp.broadcast_to(used_in[...].astype(F32), (shape[0], n_used))
    counts = jnp.where(iota(counts.shape, 1) // per_row == iota(counts.shape, 0), counts, 0.0)
    spread = jnp.where(iota((n_used, LANES), 0) % per_row == iota((n_used, LANES), 1) // slots, 1.0, 0.0)
    live = (iota(shape, 1) % slots).astype(F32) < matmul(counts.astype(BF16), spread.astype(BF16))
    fields = [
        (stamp_in[...] - g * DELTA).astype(F32),
        account_in[...].astype(F32),
        kind_in[...].astype(F32),
        jnp.where(live, weight_in[...].astype(F32), 0.0),
    ]
    for f, field in enumerate(fields):
        for shift in range(max(1, LANES // width)):
            moved = pltpu.roll(field, LANES - shift * width, 1) if shift else field
            for o in range(shift, n_dev, max(1, LANES // width)):
                at = o * width // LANES
                send[o, f * rows_per_field : (f + 1) * rows_per_field, :] = moved[at : at + rows_per_field, :]

    pltpu.make_async_copy(send.at[d], events.at[me], event_sem.at[g]).start()
    pl.semaphore_wait(barrier, devices - 1)

    def give(k):
        grp, dev = place(k)
        pltpu.make_async_remote_copy(
            send.at[dev], events.at[me], send_sem, event_sem.at[g], device_id={"grp": grp, "dev": dev}, device_id_type=MESH
        ).start()

    peers(devices, give)

    def done(ref, sem):
        pltpu.make_async_copy(ref, ref, sem).wait()

    row16, row8 = iota((16, size), 0), iota((8, size), 0)
    first, second = row16 % 4 // 2, row16 % 2
    want_before = jnp.where(row16 < 6, row16, jnp.where(row16 < 8, -1, jnp.where(row16 < 12, second, first))).astype(F32).astype(BF16)
    want_after = jnp.where(row16 < 8, -1, second).astype(F32).astype(BF16)
    want_cross = jnp.where(row16 < 6, row16, jnp.where(row16 < 8, -1, jnp.where(row16 < 12, first, -1))).astype(F32).astype(BF16)
    is_class = row16 < 8
    lane_code = iota((LANES, size), 0).astype(F32).astype(BF16)
    one, zero = jnp.ones((), BF16), jnp.zeros((), BF16)

    def tall(row):
        return jnp.concatenate([row] * (size // 16), axis=0)

    def wide(column):
        return jnp.concatenate([column] * (size // LANES), axis=1)

    profile[...] = jnp.zeros_like(profile)
    columns[...] = jnp.zeros_like(columns)
    lefts[...] = jnp.zeros_like(lefts)

    def count_range(r, carry):
        start = r * n_dev
        done(events.at[pl.ds(start, n_dev)], event_sem.at[r])
        got = []
        for h in range(rows_per_field):
            stamp, account, kind, weight = (events[pl.ds(start, n_dev), f * rows_per_field + h, :] for f in range(FIELDS))
            key = by_block(account * float(STEP) + (stamp - 8.0 * STEP), slots)
            got.append((key, by_block(kind, slots), by_block(weight, slots), jnp.transpose(key)))

        def rows_of(b):
            h, q = divmod(b, per_row)
            key, kind, weight, tall_key = got[h]
            places = [q + per_row * t for t in range(key.shape[0] // per_row)]

            def row(x):
                return jnp.concatenate([jnp.broadcast_to(x[p : p + 1, :], (16, LANES)) for p in places], axis=1)

            column = jnp.concatenate([jnp.broadcast_to(tall_key[:, p : p + 1], (LANES, LANES)) for p in places], axis=0)
            return row(key), row(kind), row(weight), column

        pick = lambda code, want, weight: jnp.where(code == want, weight, zero)
        keys = []
        for b in range(blocks):
            key, kind, weight, column = rows_of(b)
            key16 = key.astype(jnp.int32).astype(I16)
            column = column.astype(jnp.int32).astype(I16)
            keys.append(key16)
            same = tall(key16 >> 12) == wide(column >> 12)
            here, there = tall(key16), wide(column)
            before = jnp.where(same & (here > there), one, zero)
            after = jnp.where(same & (here < there), one, zero)
            turn = jnp.where(kind > 2.5, 1.0, 0.0).astype(BF16)
            kind16, weight16 = kind.astype(BF16), weight.astype(BF16)
            code = jnp.where(is_class, kind16, turn)
            sums_out[b, 0:16] = matmul(pick(code, want_before, weight16), before)
            sums_out[b, 16:24] = matmul(pick(code, want_after, weight16), after)[8:16]
            there = wide(columns[b])
            same = tall(key16 >> 12) == (there >> 12)
            cross = jnp.where(same & (here <= there), one, zero)
            sums_in[b] = matmul(lefts[b], cross)
            columns[b] = column
            lefts[b, 0:16] = pick(code, want_cross, weight16)
            account = jnp.floor(key * (1.0 / STEP)) + 8.0
            code = (kind + b) - jnp.where(kind + b > 7.5, 8.0, 0.0)
            code = (code * ACC_BLK + account).astype(BF16)
            marks[b] = jnp.where(jnp.concatenate([code] * (LANES // 16), axis=0) == lane_code, jnp.concatenate([weight16] * (LANES // 16), axis=0), zero)
        for b in range(blocks):
            here, after, cross = sums_out[b, 8:16], sums_out[b, 16:24], sums_in[b]
            pairs = sums_out[b, 0:8] + cross[0:8]
            triples = here * jnp.where(row8 < 4, cross[8:16], after) + (cross[16:24] + cross[24:32])
            left = split(jnp.concatenate([pairs, triples], axis=0))
            part = matmul_t(left, marks[b])
            profile[b] = profile[b] + (part[0:16] + part[16:32])
            chain = lefts[b, 0:16].astype(F32)[8:16] * after
            lefts[b, 16:32] = split(chain)
        return carry

    lax.fori_loop(0, n_grp, count_range, 0)

    lane = iota((16, LANES), 1) // ACC_BLK
    by_kind = []
    for c in range(6):
        x = jnp.zeros((16, LANES), F32)
        for b in range(blocks):
            x = jnp.where(lane == (b + c) % 8, profile[b], x)
        x = pltpu.roll(x, (LANES - c * ACC_BLK) % LANES, 1)
        by_kind.append(x)
        for c1 in range(6):
            out_ref[6 * c1 + c : 6 * c1 + c + 1, :] = x[c1 : c1 + 1]
    turns = [sum(by_kind[1:3], by_kind[0])[8:16], sum(by_kind[4:6], by_kind[3])[8:16]]
    out_ref[36:40, :] = jnp.zeros((4, LANES), F32)
    for d1 in range(2):
        for d2 in range(2):
            for d3 in range(2):
                at = 40 + 4 * d1 + 2 * d2 + d3
                i, j = 2 * d1 + d2, 4 + 2 * d1 + d3
                out_ref[at : at + 1, :] = turns[d3][i : i + 1] + turns[d2][j : j + 1]

    done(events.at[pl.ds(0, devices - 1)], send_sem)


def write_out(profile_ref, pair_ref, triple_ref, sems):
    pairs = pltpu.make_async_copy(profile_ref.at[pl.ds(0, 36)], pair_ref, sems.at[0])
    triples = pltpu.make_async_copy(profile_ref.at[pl.ds(40, 8)], triple_ref, sems.at[1])
    pairs.start()
    triples.start()
    pairs.wait()
    triples.wait()


def per_device(stamps, account, kind, weight, used):
    n_grp, n_dev = lax.axis_size("grp"), lax.axis_size("dev")
    blocks = used.shape[1] // n_dev
    slots = stamps.shape[0] // (n_dev * blocks)
    size = slots * n_dev
    rows = stamps.shape[0] // LANES
    chunk = FIELDS * max(1, slots * blocks // LANES)
    anywhere = pl.BlockSpec(memory_space=pl.ANY)
    vmem = pl.BlockSpec(memory_space=pltpu.VMEM)
    profile = pl.pallas_call(
        functools.partial(kernel, n_grp, n_dev, blocks, slots),
        out_shape=pltpu.VMEM((ROWS, LANES), F32),
        in_specs=[anywhere] * 5,
        out_specs=vmem,
        scratch_shapes=[
            pltpu.VMEM((rows, LANES), jnp.int32),
            pltpu.VMEM((rows, LANES), jnp.int32),
            pltpu.VMEM((rows, LANES), jnp.int32),
            pltpu.VMEM((rows, LANES), BF16),
            pltpu.VMEM(used.shape, jnp.int32),
            pltpu.VMEM((n_dev, chunk, LANES), F32),
            pltpu.VMEM((n_grp * n_dev, chunk, LANES), F32),
            pltpu.VMEM((blocks, size, LANES), I16),
            pltpu.VMEM((blocks, 32, size), BF16),
            pltpu.VMEM((blocks, 32, size), F32),
            pltpu.VMEM((blocks, 24, size), F32),
            pltpu.VMEM((blocks, LANES, size), BF16),
            pltpu.VMEM((blocks, 16, LANES), F32),
            pltpu.SemaphoreType.DMA((5,)),
            pltpu.SemaphoreType.DMA,
            pltpu.SemaphoreType.DMA((n_grp,)),
        ],
        compiler_params=pltpu.CompilerParams(collective_id=0, has_side_effects=True),
    )(*(x.reshape(rows, LANES) for x in (stamps, account, kind, weight)), used)
    return tuple(
        pl.pallas_call(
            write_out,
            out_shape=[jax.ShapeDtypeStruct((36, LANES), F32), jax.ShapeDtypeStruct((8, LANES), F32)],
            in_specs=[vmem],
            out_specs=[anywhere] * 2,
            scratch_shapes=[pltpu.SemaphoreType.DMA((2,))],
        )(pltpu.with_memory_space_constraint(profile, pltpu.VMEM))
    )


def solution(mesh):
    return jax.shard_map(
        per_device,
        mesh=mesh,
        in_specs=(
            P(("grp", "dev")),
            P(("grp", "dev")),
            P(("grp", "dev")),
            P(("grp", "dev")),
            P(("grp", "dev"), None),
        ),
        out_specs=(P(None, "dev"), P(None, "dev")),
        check_vma=False,
    )
```

```python
import functools

import jax
import jax.numpy as jnp
from jax import lax
from jax.experimental import pallas as pl
from jax.experimental.pallas import tpu as pltpu
from jax.sharding import PartitionSpec as P

DELTA = 3600
ACC_BLK = 16
LANES = 128
STEP = 4096
FIELDS = 4
ROWS = 48
MESH = pl.DeviceIdType.MESH
BF16, F32, I16 = jnp.bfloat16, jnp.float32, jnp.int16


def iota(shape, dim):
    return lax.broadcasted_iota(jnp.int32, shape, dim)


def matmul(a, b):
    return jnp.dot(a, b, preferred_element_type=F32)


def matmul_t(a, b):
    return lax.dot_general(a, b, (((1,), (1,)), ((), ())), preferred_element_type=F32)


def split(x):
    high = x.astype(BF16)
    return jnp.concatenate([high, (x - high.astype(F32)).astype(BF16)], axis=0)


def by_block(x, slots):
    senders = x.shape[0]
    per_row = LANES // slots
    row, place = iota(x.shape, 0), iota(x.shape, 1) // slots
    out = x
    for r in range(1, per_row):
        moved = pltpu.roll(pltpu.roll(x, r * slots, 1), (senders - r) % senders, 0)
        out = jnp.where((row + r - place) % per_row == 0, moved, out)
    return out


def kernel(
    n_grp, n_dev, blocks, slots,
    stamp_ref, account_ref, kind_ref, weight_ref, used_ref, out_ref,
    stamp_in, account_in, kind_in, weight_in, used_in, send, events, keys, columns, lefts, sums, crosses, marks, profile,
    in_sem, send_sem, event_sem, here_sem,
):
    g, d = lax.axis_index("grp"), lax.axis_index("dev")
    me = g * n_dev + d
    width = slots * blocks
    rows_per_field = max(1, width // LANES)
    per_row = LANES // slots
    size = slots * n_dev
    devices = n_grp * n_dev

    loads = [
        pltpu.make_async_copy(src, dst, in_sem.at[i])
        for i, (src, dst) in enumerate(
            [(stamp_ref, stamp_in), (account_ref, account_in), (kind_ref, kind_in), (weight_ref, weight_in), (used_ref, used_in)]
        )
    ]
    for load in loads:
        load.start()

    def grid(to):
        return {"grp": to // n_dev, "dev": lax.rem(to, n_dev)}

    barrier = pltpu.get_barrier_semaphore()

    @pl.loop(me + 1, devices)
    def _(to):
        pl.semaphore_signal(barrier, inc=1, device_id=grid(to), device_id_type=MESH)

    @pl.when(me > 0)
    def _():
        pl.semaphore_wait(barrier, me)

    @pl.loop(0, me)
    def _(to):
        pl.semaphore_signal(here_sem.at[g], inc=1, device_id=grid(to), device_id_type=MESH)

    for load in loads:
        load.wait()

    n_used = used_in.shape[1]
    shape = stamp_in.shape
    counts = jnp.broadcast_to(used_in[...].astype(F32), (shape[0], n_used))
    counts = jnp.where(iota(counts.shape, 1) // per_row == iota(counts.shape, 0), counts, 0.0)
    spread = jnp.where(iota((n_used, LANES), 0) % per_row == iota((n_used, LANES), 1) // slots, 1.0, 0.0)
    live = (iota(shape, 1) % slots).astype(F32) < matmul(counts.astype(BF16), spread.astype(BF16))
    fields = [
        (stamp_in[...] - g * DELTA).astype(F32),
        account_in[...].astype(F32),
        kind_in[...].astype(F32),
        jnp.where(live, weight_in[...].astype(F32), 0.0),
    ]
    for f, field in enumerate(fields):
        for shift in range(max(1, LANES // width)):
            moved = pltpu.roll(field, LANES - shift * width, 1) if shift else field
            for o in range(shift, n_dev, max(1, LANES // width)):
                at = o * width // LANES
                send[o, f * rows_per_field : (f + 1) * rows_per_field, :] = moved[at : at + rows_per_field, :]

    pltpu.make_async_copy(send.at[d], events.at[me], event_sem.at[g]).start()

    def give(to):
        pltpu.make_async_remote_copy(
            send.at[lax.rem(to, n_dev)], events.at[me], send_sem, event_sem.at[g], device_id=grid(to), device_id_type=MESH
        ).start()

    pl.loop(0, me)(give)

    def give_range(x):
        begin = jnp.maximum(x * n_dev, me + 1)
        end = (x + 1) * n_dev

        @pl.when(begin < end)
        def _():
            pl.semaphore_wait(here_sem.at[x], end - begin)
            pl.loop(begin, end)(give)

    give_range(g)

    @pl.when(g > 0)
    def _():
        pl.loop(g + 1, n_grp)(give_range)

    def done(ref, sem):
        pltpu.make_async_copy(ref, ref, sem).wait()

    row16, row8 = iota((16, size), 0), iota((8, size), 0)
    first, second = row16 % 4 // 2, row16 % 2
    want_before = jnp.where(row16 < 6, row16, jnp.where(row16 < 8, -1, jnp.where(row16 < 12, second, first))).astype(F32).astype(BF16)
    want_after = jnp.where(row16 < 8, -1, second).astype(F32).astype(BF16)
    want_cross = jnp.where(row16 < 6, row16, jnp.where(row16 < 8, -1, jnp.where(row16 < 12, first, -1))).astype(F32).astype(BF16)
    is_class = row16 < 8
    lane_code = iota((LANES, size), 0).astype(F32).astype(BF16)
    one, zero = jnp.ones((), BF16), jnp.zeros((), BF16)

    def tall(row):
        return jnp.concatenate([row] * (size // 16), axis=0)

    def wide(column):
        return jnp.concatenate([column] * (size // LANES), axis=1)

    profile[...] = jnp.zeros_like(profile)
    columns[...] = jnp.zeros_like(columns)

    def pick(code, want, weight):
        return jnp.where(code == want, weight, zero)

    def inside(r):
        slot = lax.rem(r, 2)
        begin = r * n_dev
        done(events.at[pl.ds(begin, n_dev)], event_sem.at[r])
        got = []
        for h in range(rows_per_field):
            stamp, account, kind, weight = (events[pl.ds(begin, n_dev), f * rows_per_field + h, :] for f in range(FIELDS))
            key = by_block(account * float(STEP) + (stamp - 8.0 * STEP), slots)
            got.append((key, by_block(kind, slots), by_block(weight, slots), jnp.transpose(key).astype(jnp.int32).astype(I16)))
        for b in range(blocks):
            h, q = divmod(b, per_row)
            places = [q + per_row * t for t in range(size // LANES)]
            key, kind, weight = (
                jnp.concatenate([jnp.broadcast_to(x[p : p + 1, :], (16, LANES)) for p in places], axis=1) for x in got[h][:3]
            )
            column = jnp.concatenate([jnp.broadcast_to(got[h][3][:, p : p + 1], (LANES, LANES)) for p in places], axis=0)
            key16 = key.astype(jnp.int32).astype(I16)
            same = tall(key16 >> 12) == wide(column >> 12)
            here, there = tall(key16), wide(column)
            before = jnp.where(same & (here > there), one, zero)
            after = jnp.where(same & (here < there), one, zero)
            turn = jnp.where(kind > 2.5, 1.0, 0.0).astype(BF16)
            kind16, weight16 = kind.astype(BF16), weight.astype(BF16)
            code = jnp.where(is_class, kind16, turn)
            sums_before = matmul(pick(code, want_before, weight16), before)
            sums_after = matmul(pick(code, want_after, weight16), after)[8:16]
            left = pick(code, want_cross, weight16)
            keys[slot, b] = key16
            columns[slot, b] = column
            lefts[slot, b, 0:16] = left
            sums[slot, b, 0:16] = sums_before
            sums[slot, b, 16:24] = sums_after
            account = jnp.floor(key * (1.0 / STEP)) + 8.0
            turned = (kind + b) - jnp.where(kind + b > 7.5, 8.0, 0.0)
            code = tall_mark((turned * ACC_BLK + account).astype(BF16))
            marks[slot, b] = jnp.where(code == lane_code, tall_mark(weight16), zero)
        for b in range(blocks):
            lefts[slot, b, 16:32] = split(lefts[slot, b, 0:16].astype(F32)[8:16] * sums[slot, b, 16:24])

    def tall_mark(row):
        return jnp.concatenate([row] * (LANES // 16), axis=0)

    def across(r):
        slot = lax.rem(r, 2)
        other = 1 - slot
        for b in range(blocks):
            key16, column = keys[slot, b], columns[other, b]
            same = tall(key16 >> 12) == wide(column >> 12)
            cross = jnp.where(same & (tall(key16) <= wide(column)), one, zero)
            crosses[b] = matmul(jnp.where(r > 0, lefts[other, b], zero), cross)
        for b in range(blocks):
            here, after, cross = sums[slot, b, 8:16], sums[slot, b, 16:24], crosses[b]
            pairs = sums[slot, b, 0:8] + cross[0:8]
            triples = here * jnp.where(row8 < 4, cross[8:16], after) + (cross[16:24] + cross[24:32])
            part = matmul_t(split(jnp.concatenate([pairs, triples], axis=0)), marks[slot, b])
            profile[b] = profile[b] + (part[0:16] + part[16:32])

    up = 2 * g < n_grp

    @pl.loop(0, n_grp + 1)
    def _(step):
        @pl.when((g == 0) & (step + 1 < n_grp))
        def _():
            give_range(step + 1)

        @pl.when(step < n_grp)
        def _():
            inside(jnp.where(up, step, n_grp - 1 - step))

        @pl.when(jnp.where(up, step < n_grp, step > 0))
        def _():
            across(jnp.where(up, step, n_grp - step))

    lane = iota((16, LANES), 1) // ACC_BLK
    by_kind = []
    for c in range(6):
        x = jnp.zeros((16, LANES), F32)
        for b in range(blocks):
            x = jnp.where(lane == (b + c) % 8, profile[b], x)
        x = pltpu.roll(x, (LANES - c * ACC_BLK) % LANES, 1)
        by_kind.append(x)
        for c1 in range(6):
            out_ref[6 * c1 + c : 6 * c1 + c + 1, :] = x[c1 : c1 + 1]
    turns = [sum(by_kind[1:3], by_kind[0])[8:16], sum(by_kind[4:6], by_kind[3])[8:16]]
    out_ref[36:40, :] = jnp.zeros((4, LANES), F32)
    for d1 in range(2):
        for d2 in range(2):
            for d3 in range(2):
                at = 40 + 4 * d1 + 2 * d2 + d3
                i, j = 2 * d1 + d2, 4 + 2 * d1 + d3
                out_ref[at : at + 1, :] = turns[d3][i : i + 1] + turns[d2][j : j + 1]

    done(events.at[pl.ds(0, devices - 1)], send_sem)


def write_out(profile_ref, pair_ref, triple_ref, sems):
    pairs = pltpu.make_async_copy(profile_ref.at[pl.ds(0, 36)], pair_ref, sems.at[0])
    triples = pltpu.make_async_copy(profile_ref.at[pl.ds(40, 8)], triple_ref, sems.at[1])
    pairs.start()
    triples.start()
    pairs.wait()
    triples.wait()


def per_device(stamps, account, kind, weight, used):
    n_grp, n_dev = lax.axis_size("grp"), lax.axis_size("dev")
    blocks = used.shape[1] // n_dev
    slots = stamps.shape[0] // (n_dev * blocks)
    size = slots * n_dev
    rows = stamps.shape[0] // LANES
    chunk = FIELDS * max(1, slots * blocks // LANES)
    anywhere = pl.BlockSpec(memory_space=pl.ANY)
    vmem = pl.BlockSpec(memory_space=pltpu.VMEM)
    profile = pl.pallas_call(
        functools.partial(kernel, n_grp, n_dev, blocks, slots),
        out_shape=pltpu.VMEM((ROWS, LANES), F32),
        in_specs=[anywhere] * 5,
        out_specs=vmem,
        scratch_shapes=[
            pltpu.VMEM((rows, LANES), jnp.int32),
            pltpu.VMEM((rows, LANES), jnp.int32),
            pltpu.VMEM((rows, LANES), jnp.int32),
            pltpu.VMEM((rows, LANES), BF16),
            pltpu.VMEM(used.shape, jnp.int32),
            pltpu.VMEM((n_dev, chunk, LANES), F32),
            pltpu.VMEM((n_grp * n_dev, chunk, LANES), F32),
            pltpu.VMEM((2, blocks, 16, size), I16),
            pltpu.VMEM((2, blocks, size, LANES), I16),
            pltpu.VMEM((2, blocks, 32, size), BF16),
            pltpu.VMEM((2, blocks, 24, size), F32),
            pltpu.VMEM((blocks, 32, size), F32),
            pltpu.VMEM((2, blocks, LANES, size), BF16),
            pltpu.VMEM((blocks, 16, LANES), F32),
            pltpu.SemaphoreType.DMA((5,)),
            pltpu.SemaphoreType.DMA,
            pltpu.SemaphoreType.DMA((n_grp,)),
            pltpu.SemaphoreType.REGULAR((n_grp,)),
        ],
        compiler_params=pltpu.CompilerParams(collective_id=0, has_side_effects=True),
    )(*(x.reshape(rows, LANES) for x in (stamps, account, kind, weight)), used)
    return tuple(
        pl.pallas_call(
            write_out,
            out_shape=[jax.ShapeDtypeStruct((36, LANES), F32), jax.ShapeDtypeStruct((8, LANES), F32)],
            in_specs=[vmem],
            out_specs=[anywhere] * 2,
            scratch_shapes=[pltpu.SemaphoreType.DMA((2,))],
        )(pltpu.with_memory_space_constraint(profile, pltpu.VMEM))
    )


def solution(mesh):
    return jax.shard_map(
        per_device,
        mesh=mesh,
        in_specs=(
            P(("grp", "dev")),
            P(("grp", "dev")),
            P(("grp", "dev")),
            P(("grp", "dev")),
            P(("grp", "dev"), None),
        ),
        out_specs=(P(None, "dev"), P(None, "dev")),
        check_vma=False,
    )
```

```python
import functools

import jax
import jax.numpy as jnp
from jax import lax
from jax.experimental import pallas as pl
from jax.experimental.pallas import tpu as pltpu
from jax.sharding import PartitionSpec as P

DELTA = 3600
ACC_BLK = 16
LANES = 128
STEP = 4096
FIELDS = 4
ROWS = 48
MESH = pl.DeviceIdType.MESH
BF16, F32, I16 = jnp.bfloat16, jnp.float32, jnp.int16


def iota(shape, dim):
    return lax.broadcasted_iota(jnp.int32, shape, dim)


def matmul(a, b):
    return jnp.dot(a, b, preferred_element_type=F32)


def matmul_t(a, b):
    return lax.dot_general(a, b, (((1,), (1,)), ((), ())), preferred_element_type=F32)


def split(x):
    high = x.astype(BF16)
    return jnp.concatenate([high, (x - high.astype(F32)).astype(BF16)], axis=0)


def by_block(x, slots):
    senders = x.shape[0]
    per_row = LANES // slots
    row, place = iota(x.shape, 0), iota(x.shape, 1) // slots
    out = x
    for r in range(1, per_row):
        moved = pltpu.roll(pltpu.roll(x, r * slots, 1), (senders - r) % senders, 0)
        out = jnp.where((row + r - place) % per_row == 0, moved, out)
    return out


def kernel(
    n_grp, n_dev, blocks, slots,
    stamp_ref, account_ref, kind_ref, weight_ref, used_ref, out_ref,
    stamp_in, account_in, kind_in, weight_in, used_in, send, events, columns, lefts, sums, crosses, marks, profile,
    in_sem, send_sem, event_sem, here_sem,
):
    g, d = lax.axis_index("grp"), lax.axis_index("dev")
    me = g * n_dev + d
    width = slots * blocks
    rows_per_field = max(1, width // LANES)
    per_row = LANES // slots
    size = slots * n_dev
    devices = n_grp * n_dev

    loads = [
        pltpu.make_async_copy(src, dst, in_sem.at[i])
        for i, (src, dst) in enumerate(
            [(stamp_ref, stamp_in), (account_ref, account_in), (kind_ref, kind_in), (weight_ref, weight_in), (used_ref, used_in)]
        )
    ]
    for load in loads:
        load.start()

    def grid(to):
        return {"grp": to // n_dev, "dev": lax.rem(to, n_dev)}

    barrier = pltpu.get_barrier_semaphore()

    @pl.loop(me + 1, devices)
    def _(to):
        pl.semaphore_signal(barrier, inc=1, device_id=grid(to), device_id_type=MESH)

    @pl.when(me > 0)
    def _():
        pl.semaphore_wait(barrier, me)

    @pl.loop(0, me)
    def _(to):
        pl.semaphore_signal(here_sem.at[g], inc=1, device_id=grid(to), device_id_type=MESH)

    for load in loads:
        load.wait()

    n_used = used_in.shape[1]
    shape = stamp_in.shape
    counts = jnp.broadcast_to(used_in[...].astype(F32), (shape[0], n_used))
    counts = jnp.where(iota(counts.shape, 1) // per_row == iota(counts.shape, 0), counts, 0.0)
    spread = jnp.where(iota((n_used, LANES), 0) % per_row == iota((n_used, LANES), 1) // slots, 1.0, 0.0)
    live = (iota(shape, 1) % slots).astype(F32) < matmul(counts.astype(BF16), spread.astype(BF16))
    fields = [
        (stamp_in[...] - g * DELTA).astype(F32),
        account_in[...].astype(F32),
        kind_in[...].astype(F32),
        jnp.where(live, weight_in[...].astype(F32), 0.0),
    ]
    for f, field in enumerate(fields):
        for shift in range(max(1, LANES // width)):
            moved = pltpu.roll(field, LANES - shift * width, 1) if shift else field
            for o in range(shift, n_dev, max(1, LANES // width)):
                at = o * width // LANES
                send[o, f * rows_per_field : (f + 1) * rows_per_field, :] = moved[at : at + rows_per_field, :]

    pltpu.make_async_copy(send.at[d], events.at[me], event_sem.at[g]).start()

    def give(to):
        pltpu.make_async_remote_copy(
            send.at[lax.rem(to, n_dev)], events.at[me], send_sem, event_sem.at[g], device_id=grid(to), device_id_type=MESH
        ).start()

    pl.loop(0, me)(give)

    def give_range(x):
        begin = jnp.maximum(x * n_dev, me + 1)
        end = (x + 1) * n_dev

        @pl.when(begin < end)
        def _():
            pl.semaphore_wait(here_sem.at[x], end - begin)
            pl.loop(begin, end)(give)

    give_range(g)

    @pl.when(g > 0)
    def _():
        pl.loop(g + 1, n_grp)(give_range)

    def done(ref, sem):
        pltpu.make_async_copy(ref, ref, sem).wait()

    row16, row8 = iota((16, size), 0), iota((8, size), 0)
    first, second = row16 % 4 // 2, row16 % 2
    want_before = jnp.where(row16 < 6, row16, jnp.where(row16 < 8, -1, jnp.where(row16 < 12, second, first))).astype(F32).astype(BF16)
    want_after = jnp.where(row16 < 8, -1, second).astype(F32).astype(BF16)
    want_cross = jnp.where(row16 < 6, row16, jnp.where(row16 < 8, -1, jnp.where(row16 < 12, first, -1))).astype(F32).astype(BF16)
    is_class = row16 < 8
    lane_code = iota((LANES, size), 0).astype(F32).astype(BF16)
    one, zero = jnp.ones((), BF16), jnp.zeros((), BF16)

    def tall(row):
        return jnp.concatenate([row] * (size // 16), axis=0)

    def wide(column):
        return jnp.concatenate([column] * (size // LANES), axis=1)

    profile[...] = jnp.zeros_like(profile)
    columns[...] = jnp.zeros_like(columns)
    lefts[...] = jnp.zeros_like(lefts)

    def pick(code, want, weight):
        return jnp.where(code == want, weight, zero)

    def tall_mark(row):
        return jnp.concatenate([row] * (LANES // 16), axis=0)

    up = 2 * g < n_grp
    sign = jnp.where(up, 1.0, -1.0)
    shift = jnp.where(up, -8.0 * STEP, DELTA - 1 - 8.0 * STEP)

    @pl.loop(0, n_grp)
    def _(step):
        @pl.when((g == 0) & (step + 1 < n_grp))
        def _():
            give_range(step + 1)

        r = jnp.where(up, step, n_grp - 1 - step)
        begin = r * n_dev
        done(events.at[pl.ds(begin, n_dev)], event_sem.at[r])
        got = []
        for h in range(rows_per_field):
            stamp, account, kind, weight = (events[pl.ds(begin, n_dev), f * rows_per_field + h, :] for f in range(FIELDS))
            key = by_block(account * float(STEP) + (stamp * sign + shift), slots)
            got.append((key, by_block(kind, slots), by_block(weight, slots), jnp.transpose(key).astype(jnp.int32).astype(I16)))
        for b in range(blocks):
            h, q = divmod(b, per_row)
            places = [q + per_row * t for t in range(size // LANES)]
            key, kind, weight = (
                jnp.concatenate([jnp.broadcast_to(x[p : p + 1, :], (16, LANES)) for p in places], axis=1) for x in got[h][:3]
            )
            column = jnp.concatenate([jnp.broadcast_to(got[h][3][:, p : p + 1], (LANES, LANES)) for p in places], axis=0)
            key16 = key.astype(jnp.int32).astype(I16)
            mine = tall(key16 >> 12)
            here, there = tall(key16), wide(column)
            same = mine == (there >> 12)
            before = jnp.where(same & (here > there), one, zero)
            after = jnp.where(same & (here < there), one, zero)
            turn = jnp.where(kind > 2.5, 1.0, 0.0).astype(BF16)
            kind16, weight16 = kind.astype(BF16), weight.astype(BF16)
            code = jnp.where(is_class, kind16, turn)
            sums[b, 0:16] = matmul(pick(code, want_before, weight16), before)
            sums[b, 16:24] = matmul(pick(code, want_after, weight16), after)[8:16]
            there = wide(columns[b])
            cross = jnp.where((mine == (there >> 12)) & (here <= there), one, zero)
            crosses[b] = matmul(lefts[b], cross)
            columns[b] = column
            lefts[b, 0:16] = pick(code, want_cross, weight16)
            account = jnp.floor(key * (1.0 / STEP)) + 8.0
            turned = (kind + b) - jnp.where(kind + b > 7.5, 8.0, 0.0)
            code = tall_mark((turned * ACC_BLK + account).astype(BF16))
            marks[b] = jnp.where(code == lane_code, tall_mark(weight16), zero)
        for b in range(blocks):
            here, after, cross = sums[b, 8:16], sums[b, 16:24], crosses[b]
            pairs = sums[b, 0:8] + cross[0:8]
            triples = here * jnp.where(row8 < 4, cross[8:16], after) + (cross[16:24] + cross[24:32])
            part = matmul_t(split(jnp.concatenate([pairs, triples], axis=0)), marks[b])
            profile[b] = profile[b] + (part[0:16] + part[16:32])
            lefts[b, 16:32] = split(lefts[b, 0:16].astype(F32)[8:16] * after)

    lane = iota((16, LANES), 1) // ACC_BLK
    by_kind = []
    for c in range(6):
        x = jnp.zeros((16, LANES), F32)
        for b in range(blocks):
            x = jnp.where(lane == (b + c) % 8, profile[b], x)
        x = pltpu.roll(x, (LANES - c * ACC_BLK) % LANES, 1)
        by_kind.append(x)
        for c1 in range(6):
            out_ref[pl.ds(jnp.where(up, 6 * c1 + c, 6 * c + c1), 1), :] = x[c1 : c1 + 1]
    turns = [sum(by_kind[1:3], by_kind[0])[8:16], sum(by_kind[4:6], by_kind[3])[8:16]]
    out_ref[36:40, :] = jnp.zeros((4, LANES), F32)
    for d1 in range(2):
        for d2 in range(2):
            for d3 in range(2):
                at = 40 + 2 * d2 + jnp.where(up, 4 * d1 + d3, 4 * d3 + d1)
                i, j = 2 * d1 + d2, 4 + 2 * d1 + d3
                out_ref[pl.ds(at, 1), :] = turns[d3][i : i + 1] + turns[d2][j : j + 1]

    done(events.at[pl.ds(0, devices - 1)], send_sem)


def write_out(profile_ref, pair_ref, triple_ref, sems):
    pairs = pltpu.make_async_copy(profile_ref.at[pl.ds(0, 36)], pair_ref, sems.at[0])
    triples = pltpu.make_async_copy(profile_ref.at[pl.ds(40, 8)], triple_ref, sems.at[1])
    pairs.start()
    triples.start()
    pairs.wait()
    triples.wait()


def per_device(stamps, account, kind, weight, used):
    n_grp, n_dev = lax.axis_size("grp"), lax.axis_size("dev")
    blocks = used.shape[1] // n_dev
    slots = stamps.shape[0] // (n_dev * blocks)
    size = slots * n_dev
    rows = stamps.shape[0] // LANES
    chunk = FIELDS * max(1, slots * blocks // LANES)
    anywhere = pl.BlockSpec(memory_space=pl.ANY)
    vmem = pl.BlockSpec(memory_space=pltpu.VMEM)
    profile = pl.pallas_call(
        functools.partial(kernel, n_grp, n_dev, blocks, slots),
        out_shape=pltpu.VMEM((ROWS, LANES), F32),
        in_specs=[anywhere] * 5,
        out_specs=vmem,
        scratch_shapes=[
            pltpu.VMEM((rows, LANES), jnp.int32),
            pltpu.VMEM((rows, LANES), jnp.int32),
            pltpu.VMEM((rows, LANES), jnp.int32),
            pltpu.VMEM((rows, LANES), BF16),
            pltpu.VMEM(used.shape, jnp.int32),
            pltpu.VMEM((n_dev, chunk, LANES), F32),
            pltpu.VMEM((n_grp * n_dev, chunk, LANES), F32),
            pltpu.VMEM((blocks, size, LANES), I16),
            pltpu.VMEM((blocks, 32, size), BF16),
            pltpu.VMEM((blocks, 24, size), F32),
            pltpu.VMEM((blocks, 32, size), F32),
            pltpu.VMEM((blocks, LANES, size), BF16),
            pltpu.VMEM((blocks, 16, LANES), F32),
            pltpu.SemaphoreType.DMA((5,)),
            pltpu.SemaphoreType.DMA,
            pltpu.SemaphoreType.DMA((n_grp,)),
            pltpu.SemaphoreType.REGULAR((n_grp,)),
        ],
        compiler_params=pltpu.CompilerParams(collective_id=0, has_side_effects=True),
    )(*(x.reshape(rows, LANES) for x in (stamps, account, kind, weight)), used)
    return tuple(
        pl.pallas_call(
            write_out,
            out_shape=[jax.ShapeDtypeStruct((36, LANES), F32), jax.ShapeDtypeStruct((8, LANES), F32)],
            in_specs=[vmem],
            out_specs=[anywhere] * 2,
            scratch_shapes=[pltpu.SemaphoreType.DMA((2,))],
        )(pltpu.with_memory_space_constraint(profile, pltpu.VMEM))
    )


def solution(mesh):
    return jax.shard_map(
        per_device,
        mesh=mesh,
        in_specs=(
            P(("grp", "dev")),
            P(("grp", "dev")),
            P(("grp", "dev")),
            P(("grp", "dev")),
            P(("grp", "dev"), None),
        ),
        out_specs=(P(None, "dev"), P(None, "dev")),
        check_vma=False,
    )
```

```python
import functools

import jax
import jax.numpy as jnp
from jax import lax
from jax.experimental import pallas as pl
from jax.experimental.pallas import tpu as pltpu
from jax.sharding import PartitionSpec as P

DELTA = 3600
ACC_BLK = 16
LANES = 128
STEP = 4096
FIELDS = 4
ROWS = 48
MESH = pl.DeviceIdType.MESH
BF16, F32, I16 = jnp.bfloat16, jnp.float32, jnp.int16


def iota(shape, dim):
    return lax.broadcasted_iota(jnp.int32, shape, dim)


def matmul(a, b):
    return jnp.dot(a, b, preferred_element_type=F32)


def matmul_t(a, b):
    return lax.dot_general(a, b, (((1,), (1,)), ((), ())), preferred_element_type=F32)


def split(x):
    high = x.astype(BF16)
    return jnp.concatenate([high, (x - high.astype(F32)).astype(BF16)], axis=0)


def by_block(x, slots):
    senders = x.shape[0]
    per_row = LANES // slots
    row, place = iota(x.shape, 0), iota(x.shape, 1) // slots
    out = x
    for r in range(1, per_row):
        moved = pltpu.roll(pltpu.roll(x, r * slots, 1), (senders - r) % senders, 0)
        out = jnp.where((row + r - place) % per_row == 0, moved, out)
    return out


def kernel(
    n_grp, n_dev, blocks, slots,
    stamp_ref, account_ref, kind_ref, weight_ref, used_ref, out_ref,
    stamp_in, account_in, kind_in, weight_in, used_in, send, events, columns, lefts, sums, crosses, marks, profile,
    in_sem, send_sem, event_sem, here_sem,
):
    g, d = lax.axis_index("grp"), lax.axis_index("dev")
    me = g * n_dev + d
    width = slots * blocks
    rows_per_field = max(1, width // LANES)
    per_row = LANES // slots
    size = slots * n_dev
    devices = n_grp * n_dev

    loads = [
        pltpu.make_async_copy(src, dst, in_sem.at[i])
        for i, (src, dst) in enumerate(
            [(stamp_ref, stamp_in), (account_ref, account_in), (kind_ref, kind_in), (weight_ref, weight_in), (used_ref, used_in)]
        )
    ]
    for load in loads:
        load.start()

    few = n_dev // 4

    def those_before(x):
        return jnp.where(x == g, d, jnp.where(x < g, n_dev, 0))

    def those_after(x):
        return those_before(x) + jnp.where(x == g, 1, 0)

    barrier = pltpu.get_barrier_semaphore()

    @pl.loop(g, n_grp)
    def _(x):
        @pl.loop(those_after(x), n_dev)
        def _(to):
            pl.semaphore_signal(barrier, inc=1, device_id={"grp": x, "dev": to}, device_id_type=MESH)

    @pl.when(me > 0)
    def _():
        pl.semaphore_wait(barrier, me)

    @pl.loop(0, g + 1)
    def _(x):
        @pl.loop(0, those_before(x))
        def _(to):
            pl.semaphore_signal(here_sem.at[g], inc=1, device_id={"grp": x, "dev": to}, device_id_type=MESH)

    for load in loads:
        load.wait()

    n_used = used_in.shape[1]
    shape = stamp_in.shape
    counts = jnp.broadcast_to(used_in[...].astype(F32), (shape[0], n_used))
    counts = jnp.where(iota(counts.shape, 1) // per_row == iota(counts.shape, 0), counts, 0.0)
    spread = jnp.where(iota((n_used, LANES), 0) % per_row == iota((n_used, LANES), 1) // slots, 1.0, 0.0)
    live = (iota(shape, 1) % slots).astype(F32) < matmul(counts.astype(BF16), spread.astype(BF16))
    fields = [
        (stamp_in[...] - g * DELTA).astype(F32),
        account_in[...].astype(F32),
        kind_in[...].astype(F32),
        jnp.where(live, weight_in[...].astype(F32), 0.0),
    ]
    for f, field in enumerate(fields):
        for shift in range(max(1, LANES // width)):
            moved = pltpu.roll(field, LANES - shift * width, 1) if shift else field
            for o in range(shift, n_dev, max(1, LANES // width)):
                at = o * width // LANES
                send[o, f * rows_per_field : (f + 1) * rows_per_field, :] = moved[at : at + rows_per_field, :]

    pltpu.make_async_copy(send.at[d], events.at[me], event_sem.at[g]).start()

    def give(x, begin, end):
        @pl.loop(begin, end)
        def _(to):
            pltpu.make_async_remote_copy(
                send.at[to], events.at[me], send_sem, event_sem.at[g], device_id={"grp": x, "dev": to}, device_id_type=MESH
            ).start()

    def give_after(x):
        begin = those_after(x)

        @pl.when(begin < n_dev)
        def _():
            pl.semaphore_wait(here_sem.at[x], n_dev - begin)
            give(x, begin, n_dev)

    @pl.loop(0, g + 1)
    def _(x):
        give(x, 0, those_before(x))

    @pl.loop(g, jnp.where(g == 0, 1, n_grp))
    def _(x):
        give_after(x)

    def done(ref, sem):
        pltpu.make_async_copy(ref, ref, sem).wait()

    row16, row8 = iota((16, size), 0), iota((8, size), 0)
    first, second = row16 % 4 // 2, row16 % 2
    want_before = jnp.where(row16 < 6, row16, jnp.where(row16 < 8, -1, jnp.where(row16 < 12, second, first))).astype(F32).astype(BF16)
    want_after = jnp.where(row16 < 8, -1, second).astype(F32).astype(BF16)
    want_cross = jnp.where(row16 < 6, row16, jnp.where(row16 < 8, -1, jnp.where(row16 < 12, first, -1))).astype(F32).astype(BF16)
    is_class = row16 < 8
    lane_code = iota((LANES, size), 0).astype(F32).astype(BF16)
    one, zero = jnp.ones((), BF16), jnp.zeros((), BF16)

    def tall(row):
        return jnp.concatenate([row] * (size // 16), axis=0)

    def wide(column):
        return jnp.concatenate([column] * (size // LANES), axis=1)

    profile[...] = jnp.zeros_like(profile)
    columns[...] = jnp.zeros_like(columns)
    lefts[...] = jnp.zeros_like(lefts)

    def pick(code, want, weight):
        return jnp.where(code == want, weight, zero)

    def tall_mark(row):
        return jnp.concatenate([row] * (LANES // 16), axis=0)

    up = 2 * g < n_grp
    sign = jnp.where(up, 1.0, -1.0)
    shift = jnp.where(up, -8.0 * STEP, DELTA - 1 - 8.0 * STEP)

    def prepare(r):
        begin = r * n_dev
        got = []
        for h in range(rows_per_field):
            stamp, account, kind, weight = (events[pl.ds(begin, n_dev), f * rows_per_field + h, :] for f in range(FIELDS))
            key = account * float(STEP) + (stamp * sign + shift)
            got.append((by_block(key, slots), by_block(kind, slots), by_block(weight, slots), jnp.transpose(key).astype(jnp.int32).astype(I16)))
        return got

    def count(got):
        for b in range(blocks):
            h, q = divmod(b, per_row)
            places = [q + per_row * t for t in range(size // LANES)]
            key, kind, weight = (
                jnp.concatenate([jnp.broadcast_to(x[p : p + 1, :], (16, LANES)) for p in places], axis=1) for x in got[h][:3]
            )
            senders = [s for p in places for c in range(per_row) for s in range(c, n_dev, per_row) if (s - p) % n_dev < per_row]
            column = jnp.concatenate(
                [jnp.broadcast_to(got[h][3][q * slots : (q + 1) * slots, s : s + 1], (slots, LANES)) for s in senders], axis=0
            )
            key16 = key.astype(jnp.int32).astype(I16)
            mine = tall(key16 >> 12)
            here, there = tall(key16), wide(column)
            same = mine == (there >> 12)
            before = jnp.where(same & (here > there), one, zero)
            after = jnp.where(same & (here < there), one, zero)
            turn = jnp.where(kind > 2.5, 1.0, 0.0).astype(BF16)
            kind16, weight16 = kind.astype(BF16), weight.astype(BF16)
            code = jnp.where(is_class, kind16, turn)
            sums[b, 0:16] = matmul(pick(code, want_before, weight16), before)
            sums[b, 16:24] = matmul(pick(code, want_after, weight16), after)[8:16]
            there = wide(columns[b])
            cross = jnp.where((mine == (there >> 12)) & (here <= there), one, zero)
            crosses[b] = matmul(lefts[b], cross)
            columns[b] = column
            lefts[b, 0:16] = pick(code, want_cross, weight16)
            account = jnp.floor(key * (1.0 / STEP)) + 8.0
            turned = (kind + b) - jnp.where(kind + b > 7.5, 8.0, 0.0)
            code = tall_mark((turned * ACC_BLK + account).astype(BF16))
            marks[b] = jnp.where(code == lane_code, tall_mark(weight16), zero)

    def conclude():
        for b in range(blocks):
            here, after, cross = sums[b, 8:16], sums[b, 16:24], crosses[b]
            pairs = sums[b, 0:8] + cross[0:8]
            triples = here * jnp.where(row8 < 4, cross[8:16], after) + (cross[16:24] + cross[24:32])
            part = matmul_t(split(jnp.concatenate([pairs, triples], axis=0)), marks[b])
            profile[b] = profile[b] + (part[0:16] + part[16:32])
            lefts[b, 16:32] = split(lefts[b, 0:16].astype(F32)[8:16] * after)

    def turn_of(step):
        return jnp.where(up, step, n_grp - 1 - step)

    def ready(step):
        r = turn_of(step)
        done(events.at[pl.ds(r * n_dev, n_dev)], event_sem.at[r])

    in_pairs = (g > 0) & (2 * g < n_grp) & (n_grp % 2 == 0)

    @pl.when(in_pairs)
    def _():
        @pl.loop(0, n_grp // 2)
        def _(pair):
            for i in range(2):
                ready(2 * pair + i)
            for i in range(2):
                count(prepare(turn_of(2 * pair + i)))
                conclude()

    @pl.when(jnp.logical_not(in_pairs))
    def _():
        @pl.loop(0, n_grp)
        def _(step):
            @pl.when((g == 0) & (step + 1 < n_grp) & ((d < few) | (step < 2)))
            def _():
                @pl.loop(step + 1, jnp.where((d < few) | (step == 0), step + 2, n_grp))
                def _(x):
                    give_after(x)

            ready(step)
            count(prepare(turn_of(step)))
            conclude()

    lane = iota((16, LANES), 1) // ACC_BLK
    by_kind = []
    for c in range(6):
        x = jnp.zeros((16, LANES), F32)
        for b in range(blocks):
            x = jnp.where(lane == (b + c) % 8, profile[b], x)
        x = pltpu.roll(x, (LANES - c * ACC_BLK) % LANES, 1)
        by_kind.append(x)
        for c1 in range(6):
            out_ref[pl.ds(jnp.where(up, 6 * c1 + c, 6 * c + c1), 1), :] = x[c1 : c1 + 1]
    turns = [sum(by_kind[1:3], by_kind[0])[8:16], sum(by_kind[4:6], by_kind[3])[8:16]]
    out_ref[36:40, :] = jnp.zeros((4, LANES), F32)
    for d1 in range(2):
        for d2 in range(2):
            for d3 in range(2):
                at = 40 + 2 * d2 + jnp.where(up, 4 * d1 + d3, 4 * d3 + d1)
                i, j = 2 * d1 + d2, 4 + 2 * d1 + d3
                out_ref[pl.ds(at, 1), :] = turns[d3][i : i + 1] + turns[d2][j : j + 1]

    done(events.at[pl.ds(0, devices - 1)], send_sem)


def write_out(profile_ref, pair_ref, triple_ref, sems):
    pairs = pltpu.make_async_copy(profile_ref.at[pl.ds(0, 36)], pair_ref, sems.at[0])
    triples = pltpu.make_async_copy(profile_ref.at[pl.ds(40, 8)], triple_ref, sems.at[1])
    pairs.start()
    triples.start()
    pairs.wait()
    triples.wait()


def per_device(stamps, account, kind, weight, used):
    n_grp, n_dev = lax.axis_size("grp"), lax.axis_size("dev")
    blocks = used.shape[1] // n_dev
    slots = stamps.shape[0] // (n_dev * blocks)
    size = slots * n_dev
    rows = stamps.shape[0] // LANES
    chunk = FIELDS * max(1, slots * blocks // LANES)
    anywhere = pl.BlockSpec(memory_space=pl.ANY)
    vmem = pl.BlockSpec(memory_space=pltpu.VMEM)
    profile = pl.pallas_call(
        functools.partial(kernel, n_grp, n_dev, blocks, slots),
        out_shape=pltpu.VMEM((ROWS, LANES), F32),
        in_specs=[anywhere] * 5,
        out_specs=vmem,
        scratch_shapes=[
            pltpu.VMEM((rows, LANES), jnp.int32),
            pltpu.VMEM((rows, LANES), jnp.int32),
            pltpu.VMEM((rows, LANES), jnp.int32),
            pltpu.VMEM((rows, LANES), BF16),
            pltpu.VMEM(used.shape, jnp.int32),
            pltpu.VMEM((n_dev, chunk, LANES), F32),
            pltpu.VMEM((n_grp * n_dev, chunk, LANES), F32),
            pltpu.VMEM((blocks, size, LANES), I16),
            pltpu.VMEM((blocks, 32, size), BF16),
            pltpu.VMEM((blocks, 24, size), F32),
            pltpu.VMEM((blocks, 32, size), F32),
            pltpu.VMEM((blocks, LANES, size), BF16),
            pltpu.VMEM((blocks, 16, LANES), F32),
            pltpu.SemaphoreType.DMA((5,)),
            pltpu.SemaphoreType.DMA,
            pltpu.SemaphoreType.DMA((n_grp,)),
            pltpu.SemaphoreType.REGULAR((n_grp,)),
        ],
        compiler_params=pltpu.CompilerParams(collective_id=0, has_side_effects=True),
    )(*(x.reshape(rows, LANES) for x in (stamps, account, kind, weight)), used)
    return tuple(
        pl.pallas_call(
            write_out,
            out_shape=[jax.ShapeDtypeStruct((36, LANES), F32), jax.ShapeDtypeStruct((8, LANES), F32)],
            in_specs=[vmem],
            out_specs=[anywhere] * 2,
            scratch_shapes=[pltpu.SemaphoreType.DMA((2,))],
        )(pltpu.with_memory_space_constraint(profile, pltpu.VMEM))
    )


def solution(mesh):
    return jax.shard_map(
        per_device,
        mesh=mesh,
        in_specs=(
            P(("grp", "dev")),
            P(("grp", "dev")),
            P(("grp", "dev")),
            P(("grp", "dev")),
            P(("grp", "dev"), None),
        ),
        out_specs=(P(None, "dev"), P(None, "dev")),
        check_vma=False,
    )
```

```python
import functools

import jax
import jax.numpy as jnp
from jax import lax
from jax.experimental import pallas as pl
from jax.experimental.pallas import tpu as pltpu
from jax.sharding import PartitionSpec as P

DELTA = 3600
ACC_BLK = 16
LANES = 128
STEP = 4096
FIELDS = 4
ROWS = 48
MESH = pl.DeviceIdType.MESH
BF16, F32, I16 = jnp.bfloat16, jnp.float32, jnp.int16


def iota(shape, dim):
    return lax.broadcasted_iota(jnp.int32, shape, dim)


def matmul(a, b):
    return jnp.dot(a, b, preferred_element_type=F32)


def matmul_t(a, b):
    return lax.dot_general(a, b, (((1,), (1,)), ((), ())), preferred_element_type=F32)


def split(x):
    high = x.astype(BF16)
    return jnp.concatenate([high, (x - high.astype(F32)).astype(BF16)], axis=0)


def by_block(x, slots):
    senders = x.shape[0]
    per_row = LANES // slots
    row, place = iota(x.shape, 0), iota(x.shape, 1) // slots
    out = x
    for r in range(1, per_row):
        moved = pltpu.roll(pltpu.roll(x, r * slots, 1), (senders - r) % senders, 0)
        out = jnp.where((row + r - place) % per_row == 0, moved, out)
    return out


def kernel(
    n_grp, n_dev, blocks, slots,
    stamp_ref, account_ref, kind_ref, weight_ref, used_ref, out_ref,
    stamp_in, account_in, kind_in, weight_in, used_in, send, events, columns, lefts, sums, crosses, marks, profile,
    in_sem, send_sem, event_sem, here_sem,
):
    g, d = lax.axis_index("grp"), lax.axis_index("dev")
    me = g * n_dev + d
    width = slots * blocks
    rows_per_field = max(1, width // LANES)
    per_row = LANES // slots
    size = slots * n_dev
    devices = n_grp * n_dev

    loads = [
        pltpu.make_async_copy(src, dst, in_sem.at[i])
        for i, (src, dst) in enumerate(
            [(stamp_ref, stamp_in), (account_ref, account_in), (kind_ref, kind_in), (weight_ref, weight_in), (used_ref, used_in)]
        )
    ]
    for load in loads:
        load.start()

    few, half = n_dev // 4, n_grp // 2

    def those_before(x):
        return jnp.where(x == g, d, jnp.where(x < g, n_dev, 0))

    def those_after(x):
        return those_before(x) + jnp.where(x == g, 1, 0)

    barrier = pltpu.get_barrier_semaphore()

    @pl.loop(g, n_grp)
    def _(x):
        @pl.loop(those_after(x), n_dev)
        def _(to):
            pl.semaphore_signal(barrier, inc=1, device_id={"grp": x, "dev": to}, device_id_type=MESH)

    @pl.when(me > 0)
    def _():
        pl.semaphore_wait(barrier, me)

    @pl.loop(0, g + 1)
    def _(x):
        @pl.loop(0, those_before(x))
        def _(to):
            pl.semaphore_signal(here_sem.at[g], inc=1, device_id={"grp": x, "dev": to}, device_id_type=MESH)

    for load in loads:
        load.wait()

    n_used = used_in.shape[1]
    shape = stamp_in.shape
    counts = jnp.broadcast_to(used_in[...].astype(F32), (shape[0], n_used))
    counts = jnp.where(iota(counts.shape, 1) // per_row == iota(counts.shape, 0), counts, 0.0)
    spread = jnp.where(iota((n_used, LANES), 0) % per_row == iota((n_used, LANES), 1) // slots, 1.0, 0.0)
    live = (iota(shape, 1) % slots).astype(F32) < matmul(counts.astype(BF16), spread.astype(BF16))
    fields = [
        (stamp_in[...] - g * DELTA).astype(F32),
        account_in[...].astype(F32),
        kind_in[...].astype(F32),
        jnp.where(live, weight_in[...].astype(F32), 0.0),
    ]
    for f, field in enumerate(fields):
        for shift in range(max(1, LANES // width)):
            moved = pltpu.roll(field, LANES - shift * width, 1) if shift else field
            for o in range(shift, n_dev, max(1, LANES // width)):
                at = o * width // LANES
                send[o, f * rows_per_field : (f + 1) * rows_per_field, :] = moved[at : at + rows_per_field, :]

    pltpu.make_async_copy(send.at[d], events.at[me], event_sem.at[g]).start()

    def give(x, begin, end):
        @pl.loop(begin, end)
        def _(to):
            pltpu.make_async_remote_copy(
                send.at[to], events.at[me], send_sem, event_sem.at[g], device_id={"grp": x, "dev": to}, device_id_type=MESH
            ).start()

    def give_after(x):
        begin = those_after(x)

        @pl.when(begin < n_dev)
        def _():
            pl.semaphore_wait(here_sem.at[x], n_dev - begin)
            give(x, begin, n_dev)

    @pl.loop(0, g + 1)
    def _(x):
        give(x, 0, those_before(x))

    @pl.loop(g, jnp.where(g == 0, 1, n_grp))
    def _(x):
        give_after(x)

    def done(ref, sem):
        pltpu.make_async_copy(ref, ref, sem).wait()

    row16, row8 = iota((16, size), 0), iota((8, size), 0)
    first, second = row16 % 4 // 2, row16 % 2
    want_before = jnp.where(row16 < 6, row16, jnp.where(row16 < 8, -1, jnp.where(row16 < 12, second, first))).astype(F32).astype(BF16)
    want_after = jnp.where(row16 < 8, -1, second).astype(F32).astype(BF16)
    want_cross = jnp.where(row16 < 6, row16, jnp.where(row16 < 8, -1, jnp.where(row16 < 12, first, -1))).astype(F32).astype(BF16)
    is_class = row16 < 8
    lane_code = iota((LANES, size), 0).astype(F32).astype(BF16)
    one, zero = jnp.ones((), BF16), jnp.zeros((), BF16)

    def tall(row):
        return jnp.concatenate([row] * (size // 16), axis=0)

    def wide(column):
        return jnp.concatenate([column] * (size // LANES), axis=1)

    profile[...] = jnp.zeros_like(profile)
    columns[...] = jnp.zeros_like(columns)
    lefts[...] = jnp.zeros_like(lefts)

    def pick(code, want, weight):
        return jnp.where(code == want, weight, zero)

    def tall_mark(row):
        return jnp.concatenate([row] * (LANES // 16), axis=0)

    up = 2 * g < n_grp
    sign = jnp.where(up, 1.0, -1.0)
    shift = jnp.where(up, -8.0 * STEP, DELTA - 1 - 8.0 * STEP)

    def prepare(r):
        begin = r * n_dev
        got = []
        for h in range(rows_per_field):
            stamp, account, kind, weight = (events[pl.ds(begin, n_dev), f * rows_per_field + h, :] for f in range(FIELDS))
            key = account * float(STEP) + (stamp * sign + shift)
            got.append((by_block(key, slots), by_block(kind, slots), by_block(weight, slots), jnp.transpose(key).astype(jnp.int32).astype(I16)))
        return got

    def count(got):
        for b in range(blocks):
            h, q = divmod(b, per_row)
            places = [q + per_row * t for t in range(size // LANES)]
            key, kind, weight = (
                jnp.concatenate([jnp.broadcast_to(x[p : p + 1, :], (16, LANES)) for p in places], axis=1) for x in got[h][:3]
            )
            senders = [s for p in places for c in range(per_row) for s in range(c, n_dev, per_row) if (s - p) % n_dev < per_row]
            column = jnp.concatenate(
                [jnp.broadcast_to(got[h][3][q * slots : (q + 1) * slots, s : s + 1], (slots, LANES)) for s in senders], axis=0
            )
            key16 = key.astype(jnp.int32).astype(I16)
            mine = tall(key16 >> 12)
            here, there = tall(key16), wide(column)
            same = mine == (there >> 12)
            equal = jnp.where(same, one, zero)
            before = jnp.where(here > there, equal, zero)
            after = jnp.where(here < there, equal, zero)
            turn = jnp.where(kind > 2.5, 1.0, 0.0).astype(BF16)
            kind16, weight16 = kind.astype(BF16), weight.astype(BF16)
            code = jnp.where(is_class, kind16, turn)
            sums[b, 0:16] = matmul(pick(code, want_before, weight16), before)
            sums[b, 16:24] = matmul(pick(code, want_after, weight16), after)[8:16]
            there = wide(columns[b])
            cross = jnp.where(mine == (there >> 12), jnp.where(here <= there, one, zero), zero)
            crosses[b] = matmul(lefts[b], cross)
            columns[b] = column
            lefts[b, 0:16] = pick(code, want_cross, weight16)
            account = jnp.floor(key * (1.0 / STEP)) + 8.0
            turned = (kind + b) - jnp.where(kind + b > 7.5, 8.0, 0.0)
            code = tall_mark((turned * ACC_BLK + account).astype(BF16))
            marks[b] = jnp.where(code == lane_code, tall_mark(weight16), zero)

    def conclude():
        for b in range(blocks):
            here, after, cross = sums[b, 8:16], sums[b, 16:24], crosses[b]
            pairs = sums[b, 0:8] + cross[0:8]
            triples = here * jnp.where(row8 < 4, cross[8:16], after) + (cross[16:24] + cross[24:32])
            part = matmul_t(split(jnp.concatenate([pairs, triples], axis=0)), marks[b])
            profile[b] = profile[b] + (part[0:16] + part[16:32])
            lefts[b, 16:32] = split(lefts[b, 0:16].astype(F32)[8:16] * after)

    def turn_of(step):
        return jnp.where(up, step, n_grp - 1 - step)

    def ready(step):
        r = turn_of(step)
        done(events.at[pl.ds(r * n_dev, n_dev)], event_sem.at[r])

    in_pairs = (g > 0) & (3 * g < 2 * n_grp) & (n_grp % 2 == 0)

    @pl.when(in_pairs)
    def _():
        @pl.loop(0, n_grp // 2)
        def _(pair):
            for i in range(2):
                ready(2 * pair + i)
            for i in range(2):
                count(prepare(turn_of(2 * pair + i)))
                conclude()

    @pl.when(jnp.logical_not(in_pairs))
    def _():
        @pl.loop(0, n_grp)
        def _(step):
            begin = jnp.where(d < few, step + 1, jnp.where(step == 0, 1, half + 1))
            end = jnp.where(d < few, step + 2, jnp.where(step == 0, half + 1, n_grp))

            @pl.when((g == 0) & (step + 1 < n_grp) & ((d < few) | (step < 2)))
            def _():
                @pl.loop(begin, end)
                def _(x):
                    give_after(x)

            ready(step)
            count(prepare(turn_of(step)))
            conclude()

    lane = iota((16, LANES), 1) // ACC_BLK
    by_kind = []
    for c in range(6):
        x = jnp.zeros((16, LANES), F32)
        for b in range(blocks):
            x = jnp.where(lane == (b + c) % 8, profile[b], x)
        x = pltpu.roll(x, (LANES - c * ACC_BLK) % LANES, 1)
        by_kind.append(x)
        for c1 in range(6):
            out_ref[pl.ds(jnp.where(up, 6 * c1 + c, 6 * c + c1), 1), :] = x[c1 : c1 + 1]
    turns = [sum(by_kind[1:3], by_kind[0])[8:16], sum(by_kind[4:6], by_kind[3])[8:16]]
    out_ref[36:40, :] = jnp.zeros((4, LANES), F32)
    for d1 in range(2):
        for d2 in range(2):
            for d3 in range(2):
                at = 40 + 2 * d2 + jnp.where(up, 4 * d1 + d3, 4 * d3 + d1)
                i, j = 2 * d1 + d2, 4 + 2 * d1 + d3
                out_ref[pl.ds(at, 1), :] = turns[d3][i : i + 1] + turns[d2][j : j + 1]

    done(events.at[pl.ds(0, devices - 1)], send_sem)


def write_out(profile_ref, pair_ref, triple_ref, sems):
    pairs = pltpu.make_async_copy(profile_ref.at[pl.ds(0, 36)], pair_ref, sems.at[0])
    triples = pltpu.make_async_copy(profile_ref.at[pl.ds(40, 8)], triple_ref, sems.at[1])
    pairs.start()
    triples.start()
    pairs.wait()
    triples.wait()


def per_device(stamps, account, kind, weight, used):
    n_grp, n_dev = lax.axis_size("grp"), lax.axis_size("dev")
    blocks = used.shape[1] // n_dev
    slots = stamps.shape[0] // (n_dev * blocks)
    size = slots * n_dev
    rows = stamps.shape[0] // LANES
    chunk = FIELDS * max(1, slots * blocks // LANES)
    anywhere = pl.BlockSpec(memory_space=pl.ANY)
    vmem = pl.BlockSpec(memory_space=pltpu.VMEM)
    profile = pl.pallas_call(
        functools.partial(kernel, n_grp, n_dev, blocks, slots),
        out_shape=pltpu.VMEM((ROWS, LANES), F32),
        in_specs=[anywhere] * 5,
        out_specs=vmem,
        scratch_shapes=[
            pltpu.VMEM((rows, LANES), jnp.int32),
            pltpu.VMEM((rows, LANES), jnp.int32),
            pltpu.VMEM((rows, LANES), jnp.int32),
            pltpu.VMEM((rows, LANES), BF16),
            pltpu.VMEM(used.shape, jnp.int32),
            pltpu.VMEM((n_dev, chunk, LANES), F32),
            pltpu.VMEM((n_grp * n_dev, chunk, LANES), F32),
            pltpu.VMEM((blocks, size, LANES), I16),
            pltpu.VMEM((blocks, 32, size), BF16),
            pltpu.VMEM((blocks, 24, size), F32),
            pltpu.VMEM((blocks, 32, size), F32),
            pltpu.VMEM((blocks, LANES, size), BF16),
            pltpu.VMEM((blocks, 16, LANES), F32),
            pltpu.SemaphoreType.DMA((5,)),
            pltpu.SemaphoreType.DMA,
            pltpu.SemaphoreType.DMA((n_grp,)),
            pltpu.SemaphoreType.REGULAR((n_grp,)),
        ],
        compiler_params=pltpu.CompilerParams(collective_id=0, has_side_effects=True),
    )(*(x.reshape(rows, LANES) for x in (stamps, account, kind, weight)), used)
    return tuple(
        pl.pallas_call(
            write_out,
            out_shape=[jax.ShapeDtypeStruct((36, LANES), F32), jax.ShapeDtypeStruct((8, LANES), F32)],
            in_specs=[vmem],
            out_specs=[anywhere] * 2,
            scratch_shapes=[pltpu.SemaphoreType.DMA((2,))],
        )(pltpu.with_memory_space_constraint(profile, pltpu.VMEM))
    )


def solution(mesh):
    return jax.shard_map(
        per_device,
        mesh=mesh,
        in_specs=(
            P(("grp", "dev")),
            P(("grp", "dev")),
            P(("grp", "dev")),
            P(("grp", "dev")),
            P(("grp", "dev"), None),
        ),
        out_specs=(P(None, "dev"), P(None, "dev")),
        check_vma=False,
    )
```

```python
import functools

import jax
import jax.numpy as jnp
from jax import lax
from jax.experimental import pallas as pl
from jax.experimental.pallas import tpu as pltpu
from jax.sharding import PartitionSpec as P

DELTA = 3600
ACC_BLK = 16
LANES = 128
STEP = 4096
FIELDS = 4
ROWS = 48
MESH = pl.DeviceIdType.MESH
BF16, F32, I16 = jnp.bfloat16, jnp.float32, jnp.int16


def iota(shape, dim):
    return lax.broadcasted_iota(jnp.int32, shape, dim)


def matmul(a, b):
    return jnp.dot(a, b, preferred_element_type=F32)


def matmul_t(a, b):
    return lax.dot_general(a, b, (((1,), (1,)), ((), ())), preferred_element_type=F32)


def split(x):
    high = x.astype(BF16)
    return jnp.concatenate([high, (x - high.astype(F32)).astype(BF16)], axis=0)


def by_block(x, slots):
    senders = x.shape[0]
    per_row = LANES // slots
    row, place = iota(x.shape, 0), iota(x.shape, 1) // slots
    out = x
    for r in range(1, per_row):
        moved = pltpu.roll(pltpu.roll(x, r * slots, 1), (senders - r) % senders, 0)
        out = jnp.where((row + r - place) % per_row == 0, moved, out)
    return out


def kernel(
    n_grp, n_dev, blocks, slots,
    stamp_ref, account_ref, kind_ref, weight_ref, used_ref, out_ref,
    stamp_in, account_in, kind_in, weight_in, used_in, send, events, columns, lefts, sums, crosses, marks, profile,
    in_sem, send_sem, event_sem, here_sem,
):
    g, d = lax.axis_index("grp"), lax.axis_index("dev")
    me = g * n_dev + d
    width = slots * blocks
    rows_per_field = max(1, width // LANES)
    per_row = LANES // slots
    size = slots * n_dev
    devices = n_grp * n_dev

    loads = [
        pltpu.make_async_copy(src, dst, in_sem.at[i])
        for i, (src, dst) in enumerate(
            [(stamp_ref, stamp_in), (account_ref, account_in), (kind_ref, kind_in), (weight_ref, weight_in), (used_ref, used_in)]
        )
    ]
    for load in loads:
        load.start()

    few, half = n_dev // 4, n_grp // 2

    def those_before(x):
        return jnp.where(x == g, d, jnp.where(x < g, n_dev, 0))

    def those_after(x):
        return those_before(x) + jnp.where(x == g, 1, 0)

    barrier = pltpu.get_barrier_semaphore()

    @pl.loop(g, n_grp)
    def _(x):
        @pl.loop(those_after(x), n_dev)
        def _(to):
            pl.semaphore_signal(barrier, inc=1, device_id={"grp": x, "dev": to}, device_id_type=MESH)

    @pl.when(me > 0)
    def _():
        pl.semaphore_wait(barrier, me)

    @pl.loop(0, g + 1)
    def _(x):
        @pl.loop(0, those_before(x))
        def _(to):
            pl.semaphore_signal(here_sem.at[g], inc=1, device_id={"grp": x, "dev": to}, device_id_type=MESH)

    for load in loads:
        load.wait()

    n_used = used_in.shape[1]
    shape = stamp_in.shape
    counts = jnp.broadcast_to(used_in[...].astype(F32), (shape[0], n_used))
    counts = jnp.where(iota(counts.shape, 1) // per_row == iota(counts.shape, 0), counts, 0.0)
    spread = jnp.where(iota((n_used, LANES), 0) % per_row == iota((n_used, LANES), 1) // slots, 1.0, 0.0)
    live = (iota(shape, 1) % slots).astype(F32) < matmul(counts.astype(BF16), spread.astype(BF16))
    fields = [
        (stamp_in[...] - g * DELTA).astype(F32),
        account_in[...].astype(F32),
        kind_in[...].astype(F32),
        jnp.where(live, weight_in[...].astype(F32), 0.0),
    ]
    for f, field in enumerate(fields):
        for shift in range(max(1, LANES // width)):
            moved = pltpu.roll(field, LANES - shift * width, 1) if shift else field
            for o in range(shift, n_dev, max(1, LANES // width)):
                at = o * width // LANES
                send[o, f * rows_per_field : (f + 1) * rows_per_field, :] = moved[at : at + rows_per_field, :]

    pltpu.make_async_copy(send.at[d], events.at[me], event_sem.at[g]).start()

    def give(x, begin, end):
        @pl.loop(begin, end)
        def _(to):
            pltpu.make_async_remote_copy(
                send.at[to], events.at[me], send_sem, event_sem.at[g], device_id={"grp": x, "dev": to}, device_id_type=MESH
            ).start()

    def give_after(x):
        begin = those_after(x)

        @pl.when(begin < n_dev)
        def _():
            pl.semaphore_wait(here_sem.at[x], n_dev - begin)
            give(x, begin, n_dev)

    @pl.loop(0, g + 1)
    def _(x):
        give(x, 0, those_before(x))

    @pl.loop(g, jnp.where(g == 0, 1, n_grp))
    def _(x):
        give_after(x)

    def done(ref, sem):
        pltpu.make_async_copy(ref, ref, sem).wait()

    row16, row8 = iota((16, size), 0), iota((8, size), 0)
    first, second = row16 % 4 // 2, row16 % 2
    want_before = jnp.where(row16 < 6, row16, jnp.where(row16 < 8, -1, jnp.where(row16 < 12, second, first))).astype(F32).astype(BF16)
    want_after = jnp.where(row16 < 8, -1, second).astype(F32).astype(BF16)
    want_cross = jnp.where(row16 < 6, row16, jnp.where(row16 < 8, -1, jnp.where(row16 < 12, first, -1))).astype(F32).astype(BF16)
    is_class = row16 < 8
    lane_code = iota((LANES, size), 0).astype(F32).astype(BF16)
    one, zero = jnp.ones((), BF16), jnp.zeros((), BF16)

    def tall(row):
        return jnp.concatenate([row] * (size // 16), axis=0)

    def wide(column):
        return jnp.concatenate([column] * (size // LANES), axis=1)

    profile[...] = jnp.zeros_like(profile)
    columns[...] = jnp.zeros_like(columns)
    lefts[...] = jnp.zeros_like(lefts)

    def pick(code, want, weight):
        return jnp.where(code == want, weight, zero)

    def tall_mark(row):
        return jnp.concatenate([row] * (LANES // 16), axis=0)

    up = 2 * g < n_grp
    sign = jnp.where(up, 1.0, -1.0)
    shift = jnp.where(up, -8.0 * STEP, DELTA - 1 - 8.0 * STEP)

    def prepare(r):
        begin = r * n_dev
        got = []
        for h in range(rows_per_field):
            stamp, account, kind, weight = (events[pl.ds(begin, n_dev), f * rows_per_field + h, :] for f in range(FIELDS))
            key = account * float(STEP) + (stamp * sign + shift)
            got.append((by_block(key, slots), by_block(kind, slots), by_block(weight, slots), jnp.transpose(key).astype(jnp.int32).astype(I16)))
        return got

    def count(got):
        for b in range(blocks):
            h, q = divmod(b, per_row)
            places = [q + per_row * t for t in range(size // LANES)]
            key, kind, weight = (
                jnp.concatenate([jnp.broadcast_to(x[p : p + 1, :], (16, LANES)) for p in places], axis=1) for x in got[h][:3]
            )
            senders = [s for p in places for c in range(per_row) for s in range(c, n_dev, per_row) if (s - p) % n_dev < per_row]
            column = jnp.concatenate(
                [jnp.broadcast_to(got[h][3][q * slots : (q + 1) * slots, s : s + 1], (slots, LANES)) for s in senders], axis=0
            )
            key16 = key.astype(jnp.int32).astype(I16)
            mine = tall(key16 >> 12)
            here, there = tall(key16), wide(column)
            same = mine == (there >> 12)
            equal = jnp.where(same, one, zero)
            before = jnp.where(here > there, equal, zero)
            after = jnp.where(here < there, equal, zero)
            code = jnp.where(is_class, kind, jnp.where(kind > 2.5, 1.0, 0.0)).astype(BF16)
            weight16 = weight.astype(BF16)
            sums[b, 0:16] = matmul(pick(code, want_before, weight16), before)
            sums[b, 16:24] = matmul(pick(code, want_after, weight16), after)[8:16]
            there = wide(columns[b])
            cross = jnp.where(mine == (there >> 12), jnp.where(here <= there, one, zero), zero)
            crosses[b] = matmul(lefts[b], cross)
            columns[b] = column
            lefts[b, 0:16] = pick(code, want_cross, weight16)
            account = jnp.floor(key * (1.0 / STEP)) + 8.0
            turned = (kind + b) - jnp.where(kind + b > 7.5, 8.0, 0.0)
            code = tall_mark((turned * ACC_BLK + account).astype(BF16))
            marks[b] = jnp.where(code == lane_code, tall_mark(weight16), zero)

    def conclude():
        for b in range(blocks):
            here, after, cross = sums[b, 8:16], sums[b, 16:24], crosses[b]
            pairs = sums[b, 0:8] + cross[0:8]
            triples = here * jnp.where(row8 < 4, cross[8:16], after) + (cross[16:24] + cross[24:32])
            part = matmul_t(split(jnp.concatenate([pairs, triples], axis=0)), marks[b])
            profile[b] = profile[b] + (part[0:16] + part[16:32])
            lefts[b, 16:32] = split(lefts[b, 0:16].astype(F32)[8:16] * after)

    def turn_of(step):
        return jnp.where(up, step, n_grp - 1 - step)

    def ready(step):
        r = turn_of(step)
        done(events.at[pl.ds(r * n_dev, n_dev)], event_sem.at[r])

    in_pairs = (g > 0) & (3 * g < 2 * n_grp) & (n_grp % 2 == 0)

    in_fours = in_pairs & (2 * g < n_grp) & (d < few) & (n_grp % 4 == 0)

    def in_steps_of(many):
        @pl.loop(0, n_grp // many)
        def _(group):
            for i in range(many):
                ready(many * group + i)
            for i in range(many):
                count(prepare(turn_of(many * group + i)))
                conclude()

    @pl.when(in_fours)
    def _():
        in_steps_of(4)

    @pl.when(in_pairs & jnp.logical_not(in_fours))
    def _():
        in_steps_of(2)

    @pl.when(jnp.logical_not(in_pairs))
    def _():
        @pl.loop(0, n_grp)
        def _(step):
            begin = jnp.where(d < few, step + 1, jnp.where(step == 0, 1, half + 1))
            end = jnp.where(d < few, step + 2, jnp.where(step == 0, half + 1, n_grp))

            @pl.when((g == 0) & (step + 1 < n_grp) & ((d < few) | (step < 2)))
            def _():
                @pl.loop(begin, end)
                def _(x):
                    give_after(x)

            ready(step)
            count(prepare(turn_of(step)))
            conclude()

    lane = iota((16, LANES), 1) // ACC_BLK
    by_kind = []
    for c in range(6):
        x = jnp.zeros((16, LANES), F32)
        for b in range(blocks):
            x = jnp.where(lane == (b + c) % 8, profile[b], x)
        x = pltpu.roll(x, (LANES - c * ACC_BLK) % LANES, 1)
        by_kind.append(x)
        for c1 in range(6):
            out_ref[pl.ds(jnp.where(up, 6 * c1 + c, 6 * c + c1), 1), :] = x[c1 : c1 + 1]
    turns = [sum(by_kind[1:3], by_kind[0])[8:16], sum(by_kind[4:6], by_kind[3])[8:16]]
    out_ref[36:40, :] = jnp.zeros((4, LANES), F32)
    for d1 in range(2):
        for d2 in range(2):
            for d3 in range(2):
                at = 40 + 2 * d2 + jnp.where(up, 4 * d1 + d3, 4 * d3 + d1)
                i, j = 2 * d1 + d2, 4 + 2 * d1 + d3
                out_ref[pl.ds(at, 1), :] = turns[d3][i : i + 1] + turns[d2][j : j + 1]

    done(events.at[pl.ds(0, devices - 1)], send_sem)


def write_out(profile_ref, pair_ref, triple_ref, sems):
    pairs = pltpu.make_async_copy(profile_ref.at[pl.ds(0, 36)], pair_ref, sems.at[0])
    triples = pltpu.make_async_copy(profile_ref.at[pl.ds(40, 8)], triple_ref, sems.at[1])
    pairs.start()
    triples.start()
    pairs.wait()
    triples.wait()


def per_device(stamps, account, kind, weight, used):
    n_grp, n_dev = lax.axis_size("grp"), lax.axis_size("dev")
    blocks = used.shape[1] // n_dev
    slots = stamps.shape[0] // (n_dev * blocks)
    size = slots * n_dev
    rows = stamps.shape[0] // LANES
    chunk = FIELDS * max(1, slots * blocks // LANES)
    anywhere = pl.BlockSpec(memory_space=pl.ANY)
    vmem = pl.BlockSpec(memory_space=pltpu.VMEM)
    profile = pl.pallas_call(
        functools.partial(kernel, n_grp, n_dev, blocks, slots),
        out_shape=pltpu.VMEM((ROWS, LANES), F32),
        in_specs=[anywhere] * 5,
        out_specs=vmem,
        scratch_shapes=[
            pltpu.VMEM((rows, LANES), jnp.int32),
            pltpu.VMEM((rows, LANES), jnp.int32),
            pltpu.VMEM((rows, LANES), jnp.int32),
            pltpu.VMEM((rows, LANES), BF16),
            pltpu.VMEM(used.shape, jnp.int32),
            pltpu.VMEM((n_dev, chunk, LANES), F32),
            pltpu.VMEM((n_grp * n_dev, chunk, LANES), F32),
            pltpu.VMEM((blocks, size, LANES), I16),
            pltpu.VMEM((blocks, 32, size), BF16),
            pltpu.VMEM((blocks, 24, size), F32),
            pltpu.VMEM((blocks, 32, size), F32),
            pltpu.VMEM((blocks, LANES, size), BF16),
            pltpu.VMEM((blocks, 16, LANES), F32),
            pltpu.SemaphoreType.DMA((5,)),
            pltpu.SemaphoreType.DMA,
            pltpu.SemaphoreType.DMA((n_grp,)),
            pltpu.SemaphoreType.REGULAR((n_grp,)),
        ],
        compiler_params=pltpu.CompilerParams(collective_id=0, has_side_effects=True),
    )(*(x.reshape(rows, LANES) for x in (stamps, account, kind, weight)), used)
    return tuple(
        pl.pallas_call(
            write_out,
            out_shape=[jax.ShapeDtypeStruct((36, LANES), F32), jax.ShapeDtypeStruct((8, LANES), F32)],
            in_specs=[vmem],
            out_specs=[anywhere] * 2,
            scratch_shapes=[pltpu.SemaphoreType.DMA((2,))],
        )(pltpu.with_memory_space_constraint(profile, pltpu.VMEM))
    )


def solution(mesh):
    return jax.shard_map(
        per_device,
        mesh=mesh,
        in_specs=(
            P(("grp", "dev")),
            P(("grp", "dev")),
            P(("grp", "dev")),
            P(("grp", "dev")),
            P(("grp", "dev"), None),
        ),
        out_specs=(P(None, "dev"), P(None, "dev")),
        check_vma=False,
    )
```
